128 devices in a mesh: slot: 32 (over z, y, x_hi), row: 2 (over core), col: 2 (over x_lo).
Axes of the slice: x: 4 (x_hi: 2, x_lo: 2; x = x_hi * 2 + x_lo), y: 4, z: 4, core: 2. Of those that a mesh axis runs over, the one named last changes fastest.
Arguments:
- hidden: bfloat16 [32, 128, 4096], P('slot', None, 'row'), may hold values from -20 to 20
- w_query: bfloat16 [4096, 4096], P('row', 'col'), may hold values from -0.09375 to 0.09375
- key_weight: bfloat16 [4096, 1024], P('row', 'col'), may hold values from -0.09375 to 0.09375
- value_weight: bfloat16 [4096, 1024], P('row', 'col'), may hold values from -0.09375 to 0.09375
- w_out: bfloat16 [4096, 4096], P('col', 'row'), may hold values from -0.09375 to 0.09375
- kv_store: bfloat16 [8192, 2, 8, 1024], P(('slot', 'row'), None, None, 'col'), may hold values from -250 to 250
- stretch_offset: int32 [8192], replicated, may hold values from 0 to 4095
- tile_stretch: int32 [32, 256], replicated, may hold values from 0 to 8191, as said below
- slot_count: int32 [32], replicated, may hold values from 160 to 256, as said below
- recomp_pos: int32 [32, 128], P('slot'), may hold values from 0 to 2047, as said below
Outputs:
- attn_out: bfloat16 [32, 128, 4096], P('slot', 'col', 'row')
The draws below stay inside these ranges and needn't reach their ends.
Inputs may be any that keep to these rules, and one draw needn't show every extreme that they name: Within each aligned block of 128 tiles of a slot, every value of tile_stretch // 128 that occurs occurs exactly 2 times, and 64 distinct such values occur. `slot_count`: one slot uses all 256 tiles. `recomp_pos`: entry i of slot s lies in [i * q, (i + 1) * q) with q = slot_count[s] * 8 // 128.
All inputs are finite; a program needn't handle non-finite values.
Results may differ from the reference program's by a relative error of at most 0.018.
The reference program's roundings to bfloat16 on the way (of `joined_keys`, `joined_values`, `probs_low` and `attended`) count: a program that leaves them out, or rounds other values in their place, can miss the bound.
Values may be sent and summed in bfloat16 or wider, within the bound.
A program may use at most 128 MiB of HBM per device.

```python
import math
import jax
import jax.numpy as jnp
from jax import lax

MODEL_WIDTH = 4096
QUERY_HEADS = 32
KEY_VALUE_HEADS = 8
HEAD_WIDTH = 128
STRETCH_TOKENS = 8
SLOTS = 32
GROUP = 64
TILES_DEV = 128
SLOT_TILE_LIMIT = 256
STORE_STRETCHES = 8192
CAP = 2
REDONE_TOKENS = 128


def make_plan(key):
    plan_key = jax.random.fold_in(key, 11)
    count_key, full_key, owner_key, order_key, local_key, offset_key = jax.random.split(plan_key, 6)
    counts = jax.random.randint(count_key, (SLOTS,), 5 * SLOT_TILE_LIMIT // 8, SLOT_TILE_LIMIT + 1)
    full_slot = jax.random.randint(full_key, (), 0, SLOTS)
    counts = jnp.where(jnp.arange(SLOTS) == full_slot, SLOT_TILE_LIMIT, counts).astype(jnp.int32)
    distinct = TILES_DEV // CAP
    chosen = jax.vmap(lambda sub_key: jax.random.permutation(sub_key, GROUP)[:distinct])(jax.random.split(owner_key, GROUP))
    repeated = jnp.repeat(chosen, CAP, axis=1)
    shuffle = jax.vmap(lambda sub_key: jax.random.permutation(sub_key, TILES_DEV))(jax.random.split(order_key, GROUP))
    owners = jnp.take_along_axis(repeated, shuffle, axis=1)
    locals_drawn = jax.random.randint(local_key, (GROUP, TILES_DEV), 0, TILES_DEV)
    stretches = (owners * TILES_DEV + locals_drawn).reshape(SLOTS, SLOT_TILE_LIMIT).astype(jnp.int32)
    stride = counts * STRETCH_TOKENS // REDONE_TOKENS
    offsets = jax.random.randint(offset_key, (SLOTS, REDONE_TOKENS), 0, stride[:, None])
    positions = (jnp.arange(REDONE_TOKENS, dtype=jnp.int32)[None, :] * stride[:, None] + offsets).astype(jnp.int32)
    return (counts, stretches, positions)


def draw_tile_stretch(key, part):
    return make_plan(key)[1]


def draw_slot_count(key, part):
    return make_plan(key)[0]


def draw_recomp_pos(key, part):
    return make_plan(key)[2]


def draw_hidden(key, part):
    value_random_key = jax.random.fold_in(jax.random.fold_in(key, 5), 0)
    stored_values = jnp.clip(jax.random.normal(value_random_key, (SLOTS, REDONE_TOKENS, MODEL_WIDTH), jnp.float32), -5.0, 5.0)
    return stored_values.astype(jnp.bfloat16)


def draw_kv_store(key, part):
    value_random_key = jax.random.fold_in(jax.random.fold_in(key, 3), 0)
    stored_values = jnp.clip(jax.random.normal(value_random_key, (STORE_STRETCHES, 2, STRETCH_TOKENS, KEY_VALUE_HEADS * HEAD_WIDTH), jnp.float32), -4.0, 4.0)
    return stored_values.astype(jnp.bfloat16)


def touch_ends(drawn, stream_key, least, top_value):
    longest = drawn.shape.index(max(drawn.shape))
    spots = []
    for shift in (0, 1):
        where = [jax.random.randint(jax.random.fold_in(stream_key, axis), (), 0, length) for axis, length in enumerate(drawn.shape)]
        where[longest] = (where[longest] + shift) % drawn.shape[longest]
        spots.append(tuple(where))
    return drawn.at[spots[0]].set(least).at[spots[1]].set(top_value)


def level_of(stream_key, shape, shards, low, largest):
    level = 1.0
    for position, shards_of in shards:
        heights = jax.random.uniform(jax.random.fold_in(jax.random.fold_in(stream_key, 6), position), (shards_of,), jnp.float32, low / len(shards), largest / len(shards))
        level = level * jnp.repeat(jnp.exp(heights), shape[position] // shards_of).reshape((-1,) + (1,) * (len(shape) - 1 - position))
    return level


def bell_draw(own_key, shape, width, most, shards=(), kind=jnp.bfloat16):
    entries = width * jax.random.normal(own_key, shape, jnp.float32)
    if shards:
        entries = entries * level_of(own_key, shape, shards, -0.22, 0.18)
    return jnp.clip(entries, -most, most).astype(kind)


def setup_inputs(seed: int = 0) -> dict:
    streams_of = jax.random.split(jax.random.key(seed), 11)
    return {
        "hidden": draw_hidden(jax.random.fold_in(streams_of[10], 71), 0),
        "w_query": bell_draw(streams_of[1], (MODEL_WIDTH, QUERY_HEADS * HEAD_WIDTH), MODEL_WIDTH ** -0.5, 0.09375, ((0, 2), (1, 2))),
        "key_weight": bell_draw(streams_of[2], (MODEL_WIDTH, KEY_VALUE_HEADS * HEAD_WIDTH), MODEL_WIDTH ** -0.5, 0.09375, ((0, 2), (1, 2))),
        "value_weight": bell_draw(streams_of[3], (MODEL_WIDTH, KEY_VALUE_HEADS * HEAD_WIDTH), MODEL_WIDTH ** -0.5, 0.09375, ((0, 2), (1, 2))),
        "w_out": bell_draw(streams_of[4], (QUERY_HEADS * HEAD_WIDTH, MODEL_WIDTH), (QUERY_HEADS * HEAD_WIDTH) ** -0.5, 0.09375, ((0, 2), (1, 2))),
        "kv_store": draw_kv_store(jax.random.fold_in(streams_of[10], 71), 0),
        "stretch_offset": touch_ends(jax.random.randint(streams_of[6], (STORE_STRETCHES,), 0, 4096), jax.random.fold_in(streams_of[6], 1), 0, 4095).astype(jnp.int32),
        "tile_stretch": draw_tile_stretch(jax.random.fold_in(streams_of[10], 71), 0),
        "slot_count": draw_slot_count(jax.random.fold_in(streams_of[10], 71), 0),
        "recomp_pos": draw_recomp_pos(jax.random.fold_in(streams_of[10], 71), 0),
    }


NEGATIVE = -1e+30
ROPE_BASE = 500000.0

def frequencies(head_size):
    freq_index = jnp.arange(head_size // 2, dtype=jnp.float32)
    return ROPE_BASE ** (-2.0 * freq_index / head_size)

def apply_rotation(vectors, angles):
    half_dim = vectors.shape[-1] // 2
    front_half = vectors[..., :half_dim]
    back_half = vectors[..., half_dim:]
    cosine_part = jnp.cos(angles)
    sine_part = jnp.sin(angles)
    return jnp.concatenate([front_half * cosine_part - back_half * sine_part, back_half * cosine_part + front_half * sine_part], axis=-1)

def reference(hidden, w_query, key_weight, value_weight, w_out, kv_store, stretch_offset, tile_stretch, slot_count, recomp_pos):
    freq_table = frequencies(HEAD_WIDTH)
    all_weights = jnp.concatenate([w_query, key_weight, value_weight], axis=1)
    query_columns = QUERY_HEADS * HEAD_WIDTH
    key_value_columns = KEY_VALUE_HEADS * HEAD_WIDTH
    queries_per_key_head = QUERY_HEADS // KEY_VALUE_HEADS
    total_keys = SLOT_TILE_LIMIT * STRETCH_TOKENS
    score_scale = 1.0 / math.sqrt(HEAD_WIDTH)

    def one_slot(slot_args):
        tokens, stretches, used_tiles, positions = slot_args
        gathered_rows = jnp.take(kv_store, stretches, axis=0)
        key_shift = jnp.arange(SLOT_TILE_LIMIT, dtype=jnp.int32) * STRETCH_TOKENS - jnp.take(stretch_offset, stretches)
        key_angle = key_shift.astype(jnp.float32)[:, None, None, None] * freq_table
        unrotated_keys = gathered_rows[:, 0].astype(jnp.float32).reshape(SLOT_TILE_LIMIT, STRETCH_TOKENS, KEY_VALUE_HEADS, HEAD_WIDTH)
        joined_keys = apply_rotation(unrotated_keys, key_angle).astype(jnp.bfloat16).reshape(total_keys, key_value_columns)
        joined_values = gathered_rows[:, 1].reshape(total_keys, key_value_columns)
        projected_rows = jnp.dot(tokens, all_weights, preferred_element_type=jnp.float32)
        token_angle = positions.astype(jnp.float32)[:, None, None] * freq_table
        queries = apply_rotation(projected_rows[:, :query_columns].reshape(REDONE_TOKENS, QUERY_HEADS, HEAD_WIDTH), token_angle).astype(jnp.bfloat16)
        fresh_keys = apply_rotation(projected_rows[:, query_columns:query_columns + key_value_columns].reshape(REDONE_TOKENS, KEY_VALUE_HEADS, HEAD_WIDTH), token_angle).astype(jnp.bfloat16).reshape(REDONE_TOKENS, key_value_columns)
        new_values = projected_rows[:, query_columns + key_value_columns:].astype(jnp.bfloat16)
        joined_keys = joined_keys.at[positions].set(fresh_keys)
        joined_values = joined_values.at[positions].set(new_values)
        key_pos = jnp.arange(total_keys, dtype=jnp.int32)
        allowed = jnp.logical_and(key_pos[None, :] <= positions[:, None], key_pos[None, :] < used_tiles * STRETCH_TOKENS)

        def query_head_group(group_index):
            group_queries = lax.dynamic_slice_in_dim(queries, group_index * queries_per_key_head, queries_per_key_head, 1).astype(jnp.float32)
            group_keys = lax.dynamic_slice_in_dim(joined_keys, group_index * HEAD_WIDTH, HEAD_WIDTH, 1).astype(jnp.float32)
            group_values = lax.dynamic_slice_in_dim(joined_values, group_index * HEAD_WIDTH, HEAD_WIDTH, 1).astype(jnp.float32)
            scores = jnp.einsum('qjd,kd->qjk', group_queries, group_keys) * score_scale
            scores = jnp.where(allowed[:, None, :], scores, NEGATIVE)
            peak_score = lax.optimization_barrier(jnp.max(scores, axis=2, keepdims=True))
            probs = jnp.where(allowed[:, None, :], jnp.exp(scores - peak_score), 0.0)
            totals = lax.optimization_barrier(jnp.sum(probs, axis=2))
            probs_low = lax.optimization_barrier(probs.astype(jnp.bfloat16)).astype(jnp.float32)
            weighted = jnp.einsum('qjk,kd->qjd', probs_low, group_values)
            return (weighted / totals[..., None]).astype(jnp.bfloat16)
        group_count = lax.map(query_head_group, jnp.arange(KEY_VALUE_HEADS, dtype=jnp.int32))
        attended = jnp.transpose(group_count, (1, 0, 2, 3)).reshape(REDONE_TOKENS, query_columns)
        return jnp.dot(attended, w_out, preferred_element_type=jnp.float32).astype(jnp.bfloat16)
    return lax.map(one_slot, (hidden, tile_stretch, slot_count, recomp_pos))
```

```python
import functools
import math

import jax
import jax.numpy as jnp
import numpy as np
from jax import lax
from jax.experimental import pallas as pl
from jax.experimental.pallas import tpu as pltpu
from jax.sharding import PartitionSpec as P

HEAD = 128
ROPE_BASE = 500000.0
NEG = -1e30
FAR = 1 << 20
MESH = pl.DeviceIdType.MESH
SCALE = math.log2(math.e) / math.sqrt(HEAD)
f32, bf16, i32 = jnp.float32, jnp.bfloat16, jnp.int32

TOK = 128
NZ, NY, NX = 4, 4, 2
STEPS = NZ * NY * NX
CHUNK = 4
CHUNKS = STEPS // CHUNK
MSG = 32
KEYS = CHUNK * 2 * MSG


def offsets(inner, outer):
    b, c = outer % 4, outer // 4
    return inner, (inner + b) % 4, (inner + b + c) % 2


def kernel(
    hidden, w_query, key_weight, value_weight, w_out, kv_store,
    offset_in, tiles_in, count, pos_in, freq_in,
    out,
    hid, wq, wk, wv, wo, kv, offs, tiles, pos_v, freq_v,
    send, recv, ids_v, ids, turn_c, turn_s,
    part_send, part_recv, part_own,
    q, k_new, v_new, owner_sel, pos_m,
    m_s, l_s, acc, att, o_acc, o_send, o_recv,
    load_sem, small_sem, ids_sem, w_sem, self_sem, send_sem, recv_sem,
    pair_send, pair_recv, part_ssem, part_rsem, att_ssem, att_rsem, o_ssem, o_rsem,
):
    s = lax.axis_index("slot")
    r = lax.axis_index("row")
    c = lax.axis_index("col")
    z, y, x = s // (NY * NX), (s // NX) % NY, s % NX
    me = s * 2 + r
    sign = 1 - 2 * r

    def target(step):
        dz, dy, dx = offsets(step % 4, step // 4)
        return ((z + sign * dz + 4) % 4 * NY + (y + sign * dy + 4) % 4) * NX + (x + dx) % 2

    barrier = pltpu.get_barrier_semaphore()
    pl.semaphore_signal(barrier, 1, device_id={"row": 1 - r}, device_id_type=MESH)
    pl.semaphore_signal(barrier, 1, device_id={"col": 1 - c}, device_id_type=MESH)

    def greet(slot, carry):
        @pl.when(slot != s)
        def _():
            pl.semaphore_signal(barrier, 1, device_id={"slot": slot, "row": 0}, device_id_type=MESH)
            pl.semaphore_signal(barrier, 1, device_id={"slot": slot, "row": 1}, device_id_type=MESH)

        return carry

    loads = [
        pltpu.make_async_copy(tiles_in.at[:, pl.ds(0, HEAD)], tiles.at[0], small_sem.at[0]),
        pltpu.make_async_copy(tiles_in.at[:, pl.ds(HEAD, HEAD)], tiles.at[1], small_sem.at[4]),
        pltpu.make_async_copy(offset_in, offs, small_sem.at[1]),
        pltpu.make_async_copy(pos_in, pos_v, small_sem.at[2]),
        pltpu.make_async_copy(freq_in, freq_v, small_sem.at[3]),
    ]
    kv_load = pltpu.make_async_copy(kv_store, kv, load_sem.at[0])
    hid_load = pltpu.make_async_copy(hidden.at[0], hid, load_sem.at[1])
    w_loads = [
        pltpu.make_async_copy(a, b, w_sem.at[n])
        for n, (a, b) in enumerate(((w_query, wq), (key_weight, wk), (value_weight, wv), (w_out, wo)))
    ]
    for copy in loads + [kv_load, hid_load] + w_loads:
        copy.start()
    lax.fori_loop(0, STEPS, greet, 0)
    for copy in loads:
        copy.wait()

    lane = lax.broadcasted_iota(i32, (STEPS, HEAD), 1)
    mine_offs = offs[pl.ds(me, 1), :]
    freq = freq_v[...]
    half_sign = jnp.where(lax.broadcasted_iota(i32, (1, HEAD), 1) < HEAD // 2, -1.0, 1.0)
    id_rows = jnp.zeros((STEPS, HEAD), i32)
    for b in range(2):
        block = tiles[b]
        mine = (block >> 7) == me
        code = lane * HEAD + (block & 127)
        picks = (
            jnp.min(jnp.where(mine, code, FAR), axis=1, keepdims=True),
            jnp.max(jnp.where(mine, code, 0), axis=1, keepdims=True),
        )
        for k, pick in enumerate(picks):
            local, tile = pick & 127, pick >> 7
            offset = jnp.sum(jnp.where(lane == local, mine_offs, 0), axis=1, keepdims=True)
            angle = ((b * HEAD + tile) * 8 - offset).astype(f32) * freq
            turn_c[b * 2 + k] = jnp.cos(angle)
            turn_s[b * 2 + k] = jnp.sin(angle) * half_sign
            id_rows = jnp.where(lane == b * 2 + k, local, id_rows)
    ids_v[...] = id_rows
    id_copy = pltpu.make_async_copy(ids_v, ids, ids_sem)
    id_copy.start()
    id_copy.wait()
    kv_load.wait()

    def pack(step, slot):
        for b in range(2):
            for kind in range(2):
                rows = []
                for k in range(2):
                    rows.append(kv[ids[slot, b * 2 + k], kind].astype(f32))
                for h in range(4):
                    heads = []
                    for k in range(2):
                        u = rows[k][:, h * HEAD : (h + 1) * HEAD]
                        if kind == 0:
                            cosine = turn_c[b * 2 + k, pl.ds(slot, 1), :]
                            sine = turn_s[b * 2 + k, pl.ds(slot, 1), :]
                            u = u * cosine + pltpu.roll(u, HEAD // 2, axis=1) * sine
                        heads.append(u)
                    send[step * 2 + h // 2, kind, b * 16 : (b + 1) * 16, (h % 2) * HEAD : (h % 2 + 1) * HEAD] = (
                        jnp.concatenate(heads, axis=0).astype(bf16)
                    )

    pl.semaphore_wait(barrier, 2 * STEPS)

    pack(0, s)
    self_copy = pltpu.make_async_copy(send.at[r], recv.at[r], self_sem)
    self_copy.start()
    pair_copy = pltpu.make_async_remote_copy(
        send.at[1 - r], recv.at[r], pair_send, pair_recv, device_id={"row": 1 - r}, device_id_type=MESH
    )
    pair_copy.start()

    def ship(step, carry):
        slot = target(step)
        pack(step, slot)
        for row in range(2):
            pltpu.make_async_remote_copy(
                send.at[step * 2 + row],
                recv.at[step * 2 + r],
                send_sem,
                recv_sem.at[step // CHUNK],
                device_id={"slot": slot, "row": row},
                device_id_type=MESH,
            ).start()
        return carry

    lax.fori_loop(1, STEPS, ship, 0)

    hid_load.wait()
    for copy in w_loads[:3]:
        copy.wait()
    x_in = hid[...]

    def project(side, into):
        def body(n, carry):
            cols = pl.ds(pl.multiple_of(side * 1024 + n * 256, 256), 256)
            into[:, pl.ds(pl.multiple_of(n * 256, 256), 256)] = jnp.dot(
                x_in, wq[:, cols], preferred_element_type=f32
            )
            return carry

        lax.fori_loop(0, 4, body, 0)
        cols = pl.ds(pl.multiple_of(side * 256, 256), 256)
        into[:, 1024:1280] = jnp.dot(x_in, wk[:, cols], preferred_element_type=f32)
        into[:, 1280:1536] = jnp.dot(x_in, wv[:, cols], preferred_element_type=f32)

    project(1 - r, part_send)
    part_copy = pltpu.make_async_remote_copy(
        part_send, part_recv, part_ssem, part_rsem, device_id={"row": 1 - r}, device_id_type=MESH
    )
    part_copy.start()
    project(r, part_own)

    def column(row_vector):
        return jnp.transpose(jnp.broadcast_to(row_vector, (HEAD, HEAD)))

    pos_col = column(pos_v[...])
    pos_m[:, :HEAD] = pos_col
    pos_m[:, HEAD:] = pos_col
    owner_cols = [column(tiles[b, pl.ds(s, 1), :] >> 7) for b in range(2)]
    block_of = (lax.broadcasted_iota(i32, (TOK, HEAD), 1) >> 4) & 1
    picked = jnp.where(block_of == 0, owner_cols[0], owner_cols[1])
    owner_sel[:, :HEAD] = picked
    owner_sel[:, HEAD:] = picked
    token_angle = pos_col.astype(f32) * freq
    token_c = jnp.cos(token_angle)
    token_s = jnp.sin(token_angle) * half_sign

    part_copy.wait()

    def total(lo):
        return part_own[:, lo : lo + HEAD] + part_recv[:, lo : lo + HEAD]

    def turned(lo):
        u = total(lo)
        return (u * token_c + pltpu.roll(u, HEAD // 2, axis=1) * token_s).astype(bf16)

    for h in range(8):
        q[h] = turned(h * HEAD)
    for h in range(2):
        k_new[:, h * HEAD : (h + 1) * HEAD] = turned(1024 + h * HEAD)
        v_new[:, h * HEAD : (h + 1) * HEAD] = total(1280 + h * HEAD).astype(bf16)

    def scores(qh, kh, mask):
        sc = lax.dot_general(qh, kh, (((1,), (1,)), ((), ())), preferred_element_type=f32)
        return jnp.where(mask, sc * SCALE, NEG)

    fresh = lax.broadcasted_iota(i32, (TOK, TOK), 1) <= lax.broadcasted_iota(i32, (TOK, TOK), 0)
    for h in range(8):
        g = h // 4
        sc = scores(q[h], k_new[:, g * HEAD : (g + 1) * HEAD], fresh)
        peak = jnp.max(sc, axis=1, keepdims=True)
        p = jnp.exp2(sc - peak)
        m_s[h] = jnp.broadcast_to(peak, (TOK, HEAD))
        l_s[h] = jnp.broadcast_to(jnp.sum(p, axis=1, keepdims=True), (TOK, HEAD))
        acc[h] = jnp.dot(p.astype(bf16), v_new[:, g * HEAD : (g + 1) * HEAD], preferred_element_type=f32)

    limit = count[s] * 8
    lane2 = lax.broadcasted_iota(i32, (1, KEYS), 1)
    src = lane2 >> 5
    in_block, second, unit = (lane2 >> 4) & 1, (lane2 >> 3) & 1, lane2 & 7
    src_row = src & 1
    src_sign = 1 - 2 * src_row
    tile_row = lax.broadcasted_iota(i32, (TOK, KEYS), 0)

    def attend(n, carry):
        inner = src >> 1
        b, cc = n % 4, n // 4
        dz, dy, dx = inner, (inner + b) & 3, (inner + b + cc) & 1
        source = ((((z - src_sign * dz + 4) & 3) * NY + ((y - src_sign * dy + 4) & 3)) * NX + ((x + dx) & 1)) * 2 + src_row
        here = owner_sel[...] == source
        first = jnp.min(jnp.where(here, tile_row, FAR), axis=0, keepdims=True)
        last = jnp.max(jnp.where(here, tile_row, 0), axis=0, keepdims=True)
        key_pos = (in_block * HEAD + jnp.where(second == 0, first, last)) * 8 + unit
        pos = pos_m[...]
        redone = jnp.max(jnp.where(pos == key_pos, 1, 0), axis=0, keepdims=True)
        key_pos = jnp.where(jnp.logical_or(redone > 0, key_pos >= limit), FAR, key_pos)
        mask = key_pos <= pos
        for g in range(2):
            kh = recv[pl.ds(n * 8, 8), 0, :, g * HEAD : (g + 1) * HEAD].reshape(KEYS, HEAD)
            vh = recv[pl.ds(n * 8, 8), 1, :, g * HEAD : (g + 1) * HEAD].reshape(KEYS, HEAD)
            for j in range(4):
                h = g * 4 + j
                sc = scores(q[h], kh, mask)
                old = m_s[h]
                peak = jnp.maximum(old, jnp.max(sc, axis=1, keepdims=True))
                p = jnp.exp2(sc - jnp.concatenate([peak, peak], axis=1))
                shrink = jnp.exp2(old - peak)
                m_s[h] = peak
                l_s[h] = l_s[h] * shrink + jnp.sum(p, axis=1, keepdims=True)
                acc[h] = acc[h] * shrink + jnp.dot(p.astype(bf16), vh, preferred_element_type=f32)
        return carry

    def landed(first, many, sem):
        return pltpu.make_async_copy(
            recv.at[pl.ds(first, many)], recv.at[pl.ds(first, many)], sem
        )

    self_copy.wait()
    pair_copy.wait()
    for n in range(CHUNKS):
        if n == 0:
            landed(2, 6, recv_sem.at[0]).wait()
        else:
            landed(8 * n, 8, recv_sem.at[n]).wait()
        attend(n, 0)

    for h in range(8):
        att[r, :, h * HEAD : (h + 1) * HEAD] = (acc[h] / l_s[h]).astype(bf16)
    att_copy = pltpu.make_async_remote_copy(
        att.at[r], att.at[r], att_ssem, att_rsem, device_id={"row": 1 - r}, device_id_type=MESH
    )
    att_copy.start()
    w_loads[3].wait()

    def out_cols(n):
        return pl.ds(pl.multiple_of(n * 256, 256), 256)

    def first_half(n, carry):
        rows = pl.ds(pl.multiple_of(r * 1024, 1024), 1024)
        o_acc[:, out_cols(n)] = jnp.dot(att[r], wo[rows, out_cols(n)], preferred_element_type=f32)
        return carry

    lax.fori_loop(0, 8, first_half, 0)
    att_copy.wait()

    def o_copy(n):
        return pltpu.make_async_remote_copy(
            o_send.at[n], o_recv.at[n], o_ssem.at[n], o_rsem.at[n], device_id={"col": 1 - c}, device_id_type=MESH
        )

    def second_half(n, carry):
        rows = pl.ds(pl.multiple_of((1 - r) * 1024, 1024), 1024)
        o_acc[:, out_cols(n)] += jnp.dot(att[1 - r], wo[rows, out_cols(n)], preferred_element_type=f32)
        o_send[n] = o_acc[pl.ds(pl.multiple_of((1 - c) * 64, 64), 64), out_cols(n)].astype(bf16)
        o_copy(n).start()
        return carry

    lax.fori_loop(0, 8, second_half, 0)
    own_rows = pl.ds(pl.multiple_of(c * 64, 64), 64)

    def finish(n, carry):
        o_copy(n).wait()
        out[0, :, out_cols(n)] = (o_acc[own_rows, out_cols(n)] + o_recv[n].astype(f32)).astype(bf16)
        return carry

    lax.fori_loop(0, 8, finish, 0)
    pltpu.make_async_copy(send.at[pl.ds(2, 62)], send.at[pl.ds(2, 62)], send_sem).wait()


def on_device(
    hidden, w_query, key_weight, value_weight, w_out, kv_store,
    stretch_offset, tile_stretch, slot_count, recomp_pos,
):
    freq = (ROPE_BASE ** (-2.0 * np.arange(HEAD // 2, dtype=np.float32) / HEAD)).astype(np.float32)
    freq = jnp.asarray(np.concatenate([freq, freq])[None, :])
    anywhere = pl.BlockSpec(memory_space=pl.ANY)
    dma = pltpu.SemaphoreType.DMA
    return pl.pallas_call(
        kernel,
        out_shape=jax.ShapeDtypeStruct((1, 64, 2048), bf16),
        in_specs=[anywhere] * 8 + [pl.BlockSpec(memory_space=pltpu.SMEM)] + [anywhere] * 2,
        out_specs=pl.BlockSpec(memory_space=pltpu.VMEM),
        scratch_shapes=[
            pltpu.VMEM((TOK, 2048), bf16),
            pltpu.VMEM((2048, 2048), bf16),
            pltpu.VMEM((2048, 512), bf16),
            pltpu.VMEM((2048, 512), bf16),
            pltpu.VMEM((2048, 2048), bf16),
            pltpu.VMEM((128, 2, 8, 512), bf16),
            pltpu.VMEM((64, 128), i32),
            pltpu.VMEM((2, 32, 128), i32),
            pltpu.VMEM((1, 128), i32),
            pltpu.VMEM((1, 128), f32),
            pltpu.VMEM((2 * STEPS, 2, MSG, 256), bf16),
            pltpu.VMEM((2 * STEPS, 2, MSG, 256), bf16),
            pltpu.VMEM((STEPS, HEAD), i32),
            pltpu.SMEM((STEPS, HEAD), i32),
            pltpu.VMEM((4, STEPS, HEAD), f32),
            pltpu.VMEM((4, STEPS, HEAD), f32),
            pltpu.VMEM((TOK, 1536), f32),
            pltpu.VMEM((TOK, 1536), f32),
            pltpu.VMEM((TOK, 1536), f32),
            pltpu.VMEM((8, TOK, HEAD), bf16),
            pltpu.VMEM((TOK, 256), bf16),
            pltpu.VMEM((TOK, 256), bf16),
            pltpu.VMEM((TOK, KEYS), i32),
            pltpu.VMEM((TOK, KEYS), i32),
            pltpu.VMEM((8, TOK, HEAD), f32),
            pltpu.VMEM((8, TOK, HEAD), f32),
            pltpu.VMEM((8, TOK, HEAD), f32),
            pltpu.VMEM((2, TOK, 1024), bf16),
            pltpu.VMEM((TOK, 2048), f32),
            pltpu.VMEM((8, 64, 256), bf16),
            pltpu.VMEM((8, 64, 256), bf16),
            dma((2,)), dma((5,)), dma(()), dma((4,)), dma(()), dma(()), dma((CHUNKS,)),
            dma(()), dma(()), dma(()), dma(()), dma(()), dma(()), dma((8,)), dma((8,)),
        ],
        compiler_params=pltpu.CompilerParams(
            collective_id=0, has_side_effects=True, vmem_limit_bytes=58 << 20
        ),
        name="joined_attention",
    )(
        hidden, w_query, key_weight, value_weight, w_out, kv_store,
        stretch_offset.reshape(64, 128), tile_stretch, slot_count, recomp_pos, freq,
    )


def solution(mesh):
    return jax.shard_map(
        on_device,
        mesh=mesh,
        in_specs=(
            P("slot", None, "row"),
            P("row", "col"),
            P("row", "col"),
            P("row", "col"),
            P("col", "row"),
            P(("slot", "row"), None, None, "col"),
            P(),
            P(),
            P(),
            P("slot", None),
        ),
        out_specs=P("slot", "col", "row"),
        check_vma=False,
    )
```

```python
import functools
import math

import jax
import jax.numpy as jnp
import numpy as np
from jax import lax
from jax.experimental import pallas as pl
from jax.experimental.pallas import tpu as pltpu
from jax.sharding import PartitionSpec as P

HEAD = 128
ROPE_BASE = 500000.0
NEG = -1e30
FAR = 1 << 20
MESH = pl.DeviceIdType.MESH
SCALE = math.log2(math.e) / math.sqrt(HEAD)
f32, bf16, i32 = jnp.float32, jnp.bfloat16, jnp.int32

TOK = 128
NZ, NY, NX = 4, 4, 2
STEPS = NZ * NY * NX
CHUNK = 4
CHUNKS = STEPS // CHUNK
MSG = 32
KEYS = CHUNK * 2 * MSG


def offsets(inner, outer):
    b, c = outer % 4, outer // 4
    return inner, (inner + b) % 4, (inner + b + c) % 2


def kernel(
    hidden, w_query, key_weight, value_weight, w_out, kv_store,
    offset_in, tiles_in, count_in, pos_in, freq_in,
    out,
    hid, wq, wk, wv, wo, kv, offs, tiles, count, pos_v, freq_v,
    send, recv, ids_v, ids, turn_c, turn_s,
    part_send, part_recv, part_own,
    q, k_new, v_new, owner_sel, pos_m,
    m_s, l_s, acc, att, o_acc, o_send, o_recv,
    load_sem, small_sem, ids_sem, w_sem, self_sem, send_sem, recv_sem,
    pair_send, pair_recv, part_ssem, part_rsem, att_ssem, att_rsem, o_ssem, o_rsem,
):
    s = lax.axis_index("slot")
    r = lax.axis_index("row")
    c = lax.axis_index("col")
    z, y, x = s // (NY * NX), (s // NX) % NY, s % NX
    me = s * 2 + r
    sign = 1 - 2 * r

    def target(step):
        dz, dy, dx = offsets(step % 4, step // 4)
        return ((z + sign * dz + 4) % 4 * NY + (y + sign * dy + 4) % 4) * NX + (x + dx) % 2

    barrier = pltpu.get_barrier_semaphore()
    pl.semaphore_signal(barrier, 1, device_id={"row": 1 - r}, device_id_type=MESH)
    pl.semaphore_signal(barrier, 1, device_id={"col": 1 - c}, device_id_type=MESH)

    def greet(slot, carry):
        @pl.when(slot != s)
        def _():
            pl.semaphore_signal(barrier, 1, device_id={"slot": slot, "row": 0}, device_id_type=MESH)
            pl.semaphore_signal(barrier, 1, device_id={"slot": slot, "row": 1}, device_id_type=MESH)

        return carry

    loads = [
        pltpu.make_async_copy(tiles_in.at[:, pl.ds(0, HEAD)], tiles.at[0], small_sem.at[0]),
        pltpu.make_async_copy(tiles_in.at[:, pl.ds(HEAD, HEAD)], tiles.at[1], small_sem.at[4]),
        pltpu.make_async_copy(offset_in, offs, small_sem.at[1]),
        pltpu.make_async_copy(pos_in, pos_v, small_sem.at[2]),
        pltpu.make_async_copy(count_in, count, small_sem.at[5]),
        pltpu.make_async_copy(freq_in, freq_v, small_sem.at[3]),
    ]
    kv_load = pltpu.make_async_copy(kv_store, kv, load_sem.at[0])
    hid_load = pltpu.make_async_copy(hidden.at[0], hid, load_sem.at[1])
    w_loads = [
        pltpu.make_async_copy(a, b, w_sem.at[n])
        for n, (a, b) in enumerate(((w_query, wq), (key_weight, wk), (value_weight, wv), (w_out, wo)))
    ]
    for copy in loads + [kv_load]:
        copy.start()
    lax.fori_loop(0, STEPS, greet, 0)
    for copy in loads:
        copy.wait()

    lane = lax.broadcasted_iota(i32, (STEPS, HEAD), 1)
    mine_offs = offs[pl.ds(me, 1), :]
    freq = freq_v[...]
    half_sign = jnp.where(lax.broadcasted_iota(i32, (1, HEAD), 1) < HEAD // 2, -1.0, 1.0)
    id_rows = jnp.zeros((STEPS, HEAD), i32)
    for b in range(2):
        block = tiles[b]
        mine = (block >> 7) == me
        code = lane * HEAD + (block & 127)
        picks = (
            jnp.min(jnp.where(mine, code, FAR), axis=1, keepdims=True),
            jnp.max(jnp.where(mine, code, 0), axis=1, keepdims=True),
        )
        for k, pick in enumerate(picks):
            local, tile = pick & 127, pick >> 7
            offset = jnp.sum(jnp.where(lane == local, mine_offs, 0), axis=1, keepdims=True)
            angle = ((b * HEAD + tile) * 8 - offset).astype(f32) * freq
            turn_c[b * 2 + k] = jnp.cos(angle)
            turn_s[b * 2 + k] = jnp.sin(angle) * half_sign
            id_rows = jnp.where(lane == b * 2 + k, local, id_rows)
    ids_v[...] = id_rows
    id_copy = pltpu.make_async_copy(ids_v, ids, ids_sem)
    id_copy.start()
    id_copy.wait()
    kv_load.wait()
    for copy in [hid_load] + w_loads:
        copy.start()

    def pack(step, slot):
        for b in range(2):
            for kind in range(2):
                rows = []
                for k in range(2):
                    rows.append(kv[ids[slot, b * 2 + k], kind].astype(f32))
                for h in range(4):
                    heads = []
                    for k in range(2):
                        u = rows[k][:, h * HEAD : (h + 1) * HEAD]
                        if kind == 0:
                            cosine = turn_c[b * 2 + k, pl.ds(slot, 1), :]
                            sine = turn_s[b * 2 + k, pl.ds(slot, 1), :]
                            u = u * cosine + pltpu.roll(u, HEAD // 2, axis=1) * sine
                        heads.append(u)
                    send[step * 2 + h // 2, kind, b * 16 : (b + 1) * 16, (h % 2) * HEAD : (h % 2 + 1) * HEAD] = (
                        jnp.concatenate(heads, axis=0).astype(bf16)
                    )

    pl.semaphore_wait(barrier, 2 * STEPS)

    pack(0, s)
    self_copy = pltpu.make_async_copy(send.at[r], recv.at[r], self_sem)
    self_copy.start()
    pair_copy = pltpu.make_async_remote_copy(
        send.at[1 - r], recv.at[r], pair_send, pair_recv, device_id={"row": 1 - r}, device_id_type=MESH
    )
    pair_copy.start()

    def ship(step, carry):
        slot = target(step)
        pack(step, slot)
        for row in range(2):
            pltpu.make_async_remote_copy(
                send.at[step * 2 + row],
                recv.at[step * 2 + r],
                send_sem,
                recv_sem.at[step // CHUNK],
                device_id={"slot": slot, "row": row},
                device_id_type=MESH,
            ).start()
        return carry

    lax.fori_loop(1, STEPS, ship, 0)

    hid_load.wait()
    for copy in w_loads[:3]:
        copy.wait()
    x_in = hid[...]

    def project(side, into):
        def body(n, carry):
            cols = pl.ds(pl.multiple_of(side * 1024 + n * 256, 256), 256)
            into[:, pl.ds(pl.multiple_of(n * 256, 256), 256)] = jnp.dot(
                x_in, wq[:, cols], preferred_element_type=f32
            )
            return carry

        lax.fori_loop(0, 4, body, 0)
        cols = pl.ds(pl.multiple_of(side * 256, 256), 256)
        into[:, 1024:1280] = jnp.dot(x_in, wk[:, cols], preferred_element_type=f32)
        into[:, 1280:1536] = jnp.dot(x_in, wv[:, cols], preferred_element_type=f32)

    project(1 - r, part_send)
    part_copy = pltpu.make_async_remote_copy(
        part_send, part_recv, part_ssem, part_rsem, device_id={"row": 1 - r}, device_id_type=MESH
    )
    part_copy.start()
    project(r, part_own)

    def column(row_vector):
        return jnp.transpose(jnp.broadcast_to(row_vector, (HEAD, HEAD)))

    pos_col = column(pos_v[...])
    pos_m[:, :HEAD] = pos_col
    pos_m[:, HEAD:] = pos_col
    owner_cols = [column(tiles[b, pl.ds(s, 1), :] >> 7) for b in range(2)]
    block_of = (lax.broadcasted_iota(i32, (TOK, HEAD), 1) >> 4) & 1
    picked = jnp.where(block_of == 0, owner_cols[0], owner_cols[1])
    owner_sel[:, :HEAD] = picked
    owner_sel[:, HEAD:] = picked
    token_angle = pos_col.astype(f32) * freq
    token_c = jnp.cos(token_angle)
    token_s = jnp.sin(token_angle) * half_sign

    part_copy.wait()

    def total(lo):
        return part_own[:, lo : lo + HEAD] + part_recv[:, lo : lo + HEAD]

    def turned(lo):
        u = total(lo)
        return (u * token_c + pltpu.roll(u, HEAD // 2, axis=1) * token_s).astype(bf16)

    for h in range(8):
        q[h] = turned(h * HEAD)
    for h in range(2):
        k_new[:, h * HEAD : (h + 1) * HEAD] = turned(1024 + h * HEAD)
        v_new[:, h * HEAD : (h + 1) * HEAD] = total(1280 + h * HEAD).astype(bf16)

    def scores(qh, kh, mask):
        sc = lax.dot_general(qh, kh, (((1,), (1,)), ((), ())), preferred_element_type=f32)
        return jnp.where(mask, sc * SCALE, NEG)

    fresh = lax.broadcasted_iota(i32, (TOK, TOK), 1) <= lax.broadcasted_iota(i32, (TOK, TOK), 0)
    for h in range(8):
        g = h // 4
        sc = scores(q[h], k_new[:, g * HEAD : (g + 1) * HEAD], fresh)
        peak = jnp.max(sc, axis=1, keepdims=True)
        p = jnp.exp2(sc - peak)
        m_s[h] = jnp.broadcast_to(peak, (TOK, HEAD))
        l_s[h] = jnp.broadcast_to(jnp.sum(p, axis=1, keepdims=True), (TOK, HEAD))
        acc[h] = jnp.dot(p.astype(bf16), v_new[:, g * HEAD : (g + 1) * HEAD], preferred_element_type=f32)

    limit = count[s] * 8
    lane2 = lax.broadcasted_iota(i32, (1, KEYS), 1)
    src = lane2 >> 5
    in_block, second, unit = (lane2 >> 4) & 1, (lane2 >> 3) & 1, lane2 & 7
    src_row = src & 1
    src_sign = 1 - 2 * src_row
    tile_row = lax.broadcasted_iota(i32, (TOK, KEYS), 0)

    def attend(n, done=None):
        inner = src >> 1
        b, cc = n % 4, n // 4
        dz, dy, dx = inner, (inner + b) & 3, (inner + b + cc) & 1
        source = ((((z - src_sign * dz + 4) & 3) * NY + ((y - src_sign * dy + 4) & 3)) * NX + ((x + dx) & 1)) * 2 + src_row
        here = owner_sel[...] == source
        first = jnp.min(jnp.where(here, tile_row, FAR), axis=0, keepdims=True)
        last = jnp.max(jnp.where(here, tile_row, 0), axis=0, keepdims=True)
        key_pos = (in_block * HEAD + jnp.where(second == 0, first, last)) * 8 + unit
        pos = pos_m[...]
        redone = jnp.max(jnp.where(pos == key_pos, 1, 0), axis=0, keepdims=True)
        key_pos = jnp.where(jnp.logical_or(redone > 0, key_pos >= limit), FAR, key_pos)
        mask = key_pos <= pos
        for g in range(2):
            kh = recv[pl.ds(n * 8, 8), 0, :, g * HEAD : (g + 1) * HEAD].reshape(KEYS, HEAD)
            vh = recv[pl.ds(n * 8, 8), 1, :, g * HEAD : (g + 1) * HEAD].reshape(KEYS, HEAD)
            for j in range(4):
                h = g * 4 + j
                sc = scores(q[h], kh, mask)
                old = m_s[h]
                peak = jnp.maximum(old, jnp.max(sc, axis=1, keepdims=True))
                p = jnp.exp2(sc - jnp.concatenate([peak, peak], axis=1))
                shrink = jnp.exp2(old - peak)
                m_s[h] = peak
                l_s[h] = l_s[h] * shrink + jnp.sum(p, axis=1, keepdims=True)
                acc[h] = acc[h] * shrink + jnp.dot(p.astype(bf16), vh, preferred_element_type=f32)
                if done is not None:
                    done(h)

    def landed(first, many, sem):
        return pltpu.make_async_copy(
            recv.at[pl.ds(first, many)], recv.at[pl.ds(first, many)], sem
        )

    def att_copy(n):
        part = att.at[r]
        return pltpu.make_async_remote_copy(
            part, part, att_ssem.at[n], att_rsem.at[n], device_id={"row": 1 - r}, device_id_type=MESH
        )

    def share(h):
        att[r, :, h * HEAD : (h + 1) * HEAD] = (acc[h] / l_s[h]).astype(bf16)
        if h == 7:
            att_copy(0).start()

    self_copy.wait()
    pair_copy.wait()
    for n in range(CHUNKS):
        if n == 0:
            landed(2, 6, recv_sem.at[0]).wait()
        else:
            landed(8 * n, 8, recv_sem.at[n]).wait()
        attend(n)

    for h in range(8):
        share(h)
    w_loads[3].wait()

    def out_cols(n):
        return pl.ds(pl.multiple_of(n * 256, 256), 256)

    def first_half(n, carry):
        rows = pl.ds(pl.multiple_of(r * 1024, 1024), 1024)
        o_acc[:, out_cols(n)] = jnp.dot(att[r], wo[rows, out_cols(n)], preferred_element_type=f32)
        return carry

    lax.fori_loop(0, 8, first_half, 0)
    att_copy(0).wait()

    def o_copy(n):
        return pltpu.make_async_remote_copy(
            o_send.at[n], o_recv.at[n], o_ssem.at[n], o_rsem.at[n], device_id={"col": 1 - c}, device_id_type=MESH
        )

    def second_half(n, carry):
        rows = pl.ds(pl.multiple_of((1 - r) * 1024, 1024), 1024)
        o_acc[:, out_cols(n)] += jnp.dot(att[1 - r], wo[rows, out_cols(n)], preferred_element_type=f32)
        o_send[n] = o_acc[pl.ds(pl.multiple_of((1 - c) * 64, 64), 64), out_cols(n)].astype(bf16)
        o_copy(n).start()
        return carry

    own_rows = pl.ds(pl.multiple_of(c * 64, 64), 64)
    lax.fori_loop(0, 8, second_half, 0)

    def finish(n, carry):
        o_copy(n).wait()
        out[0, :, out_cols(n)] = (o_acc[own_rows, out_cols(n)] + o_recv[n].astype(f32)).astype(bf16)
        return carry

    lax.fori_loop(0, 8, finish, 0)
    pltpu.make_async_copy(send.at[pl.ds(2, 62)], send.at[pl.ds(2, 62)], send_sem).wait()


def on_device(
    hidden, w_query, key_weight, value_weight, w_out, kv_store,
    stretch_offset, tile_stretch, slot_count, recomp_pos,
):
    freq = (ROPE_BASE ** (-2.0 * np.arange(HEAD // 2, dtype=np.float32) / HEAD)).astype(np.float32)
    freq = jnp.asarray(np.concatenate([freq, freq])[None, :])
    dma = pltpu.SemaphoreType.DMA
    operands = (
        hidden, w_query, key_weight, value_weight, w_out, kv_store,
        stretch_offset.reshape(64, 128), tile_stretch, slot_count, recomp_pos, freq,
    )
    return pl.pallas_call(
        kernel,
        out_shape=jax.ShapeDtypeStruct((1, 64, 2048), bf16),
        in_specs=[pl.BlockSpec(memory_space=pltpu.HBM)] * 11,
        out_specs=pl.BlockSpec(memory_space=pltpu.VMEM),
        scratch_shapes=[
            pltpu.VMEM((TOK, 2048), bf16),
            pltpu.VMEM((2048, 2048), bf16),
            pltpu.VMEM((2048, 512), bf16),
            pltpu.VMEM((2048, 512), bf16),
            pltpu.VMEM((2048, 2048), bf16),
            pltpu.VMEM((128, 2, 8, 512), bf16),
            pltpu.VMEM((64, 128), i32),
            pltpu.VMEM((2, 32, 128), i32),
            pltpu.SMEM((32,), i32),
            pltpu.VMEM((1, 128), i32),
            pltpu.VMEM((1, 128), f32),
            pltpu.VMEM((2 * STEPS, 2, MSG, 256), bf16),
            pltpu.VMEM((2 * STEPS, 2, MSG, 256), bf16),
            pltpu.VMEM((STEPS, HEAD), i32),
            pltpu.SMEM((STEPS, HEAD), i32),
            pltpu.VMEM((4, STEPS, HEAD), f32),
            pltpu.VMEM((4, STEPS, HEAD), f32),
            pltpu.VMEM((TOK, 1536), f32),
            pltpu.VMEM((TOK, 1536), f32),
            pltpu.VMEM((TOK, 1536), f32),
            pltpu.VMEM((8, TOK, HEAD), bf16),
            pltpu.VMEM((TOK, 256), bf16),
            pltpu.VMEM((TOK, 256), bf16),
            pltpu.VMEM((TOK, KEYS), i32),
            pltpu.VMEM((TOK, KEYS), i32),
            pltpu.VMEM((8, TOK, HEAD), f32),
            pltpu.VMEM((8, TOK, HEAD), f32),
            pltpu.VMEM((8, TOK, HEAD), f32),
            pltpu.VMEM((2, TOK, 1024), bf16),
            pltpu.VMEM((TOK, 2048), f32),
            pltpu.VMEM((8, 64, 256), bf16),
            pltpu.VMEM((8, 64, 256), bf16),
            dma((2,)), dma((6,)), dma(()), dma((4,)), dma(()), dma(()), dma((CHUNKS,)),
            dma(()), dma(()), dma(()), dma(()), dma((4,)), dma((4,)), dma((8,)), dma((8,)),
        ],
        compiler_params=pltpu.CompilerParams(
            collective_id=0, has_side_effects=True, vmem_limit_bytes=44 << 20
        ),
        name="joined_attention",
    )(*(pltpu.with_memory_space_constraint(a, pltpu.HBM) for a in operands))


def solution(mesh):
    return jax.shard_map(
        on_device,
        mesh=mesh,
        in_specs=(
            P("slot", None, "row"),
            P("row", "col"),
            P("row", "col"),
            P("row", "col"),
            P("col", "row"),
            P(("slot", "row"), None, None, "col"),
            P(),
            P(),
            P(),
            P("slot", None),
        ),
        out_specs=P("slot", "col", "row"),
        check_vma=False,
    )
```

```python
import functools
import math

import jax
import jax.numpy as jnp
import numpy as np
from jax import lax
from jax.experimental import pallas as pl
from jax.experimental.pallas import tpu as pltpu
from jax.sharding import PartitionSpec as P

HEAD = 128
ROPE_BASE = 500000.0
NEG = -1e30
FAR = 1 << 20
MESH = pl.DeviceIdType.MESH
SCALE = math.log2(math.e) / math.sqrt(HEAD)
f32, bf16, i32 = jnp.float32, jnp.bfloat16, jnp.int32

TOK = 128
NZ, NY, NX = 4, 4, 2
STEPS = NZ * NY * NX
CHUNK = 4
CHUNKS = STEPS // CHUNK
MSG = 32
KEYS = CHUNK * 2 * MSG


def send_order():
    order = [(0, 0, 0)]
    for j in range(1, 4):
        order += [(j, 0, 0), (0, j, 0)]
    order += [(0, 0, 1)]
    for j in range(1, 4):
        order += [(j, 0, 1), (0, j, 1)] + [(j, 1 + (j + n) % 3, 0) for n in range(3)]
    for m in range(9):
        order += [(1 + m // 3, 1 + (m // 3 + m) % 3, 1)]
    return order


def kernel(
    hidden, w_query, key_weight, value_weight, w_out, kv_store,
    offset_in, tiles_in, count_in, pos_in, freq_in, steps_in,
    out,
    hid, wq, wk, wv, wo, kv, offs, tiles, count, pos_v, freq_v, steps_v,
    send, recv, ids_v, ids, turn_c, turn_s,
    part_send, part_recv, part_own,
    q, k_new, v_new, owner_sel, pos_m,
    m_s, l_s, acc, att, o_acc, o_send, o_recv,
    load_sem, small_sem, ids_sem, w_sem, self_sem, send_sem, recv_sem,
    pair_send, pair_recv, part_ssem, part_rsem, att_ssem, att_rsem, o_ssem, o_rsem, second_stage, third_stage,
):
    s = lax.axis_index("slot")
    r = lax.axis_index("row")
    c = lax.axis_index("col")
    z, y, x = s // (NY * NX), (s // NX) % NY, s % NX
    me = s * 2 + r
    sign = 1 - 2 * r

    def target(dz, dy, dx):
        return ((z + sign * dz + 4) % 4 * NY + (y + sign * dy + 4) % 4) * NX + (x + dx) % 2

    near = [target(j, 0, 0) for j in range(1, 4)] + [target(0, j, 0) for j in range(1, 4)] + [target(0, 0, 1)]

    barrier = pltpu.get_barrier_semaphore()
    pl.semaphore_signal(barrier, 1, device_id={"row": 1 - r}, device_id_type=MESH)
    pl.semaphore_signal(barrier, 1, device_id={"col": 1 - c}, device_id_type=MESH)
    for slot in near:
        for row in range(2):
            pl.semaphore_signal(barrier, 1, device_id={"slot": slot, "row": row}, device_id_type=MESH)

    def tell(stage):
        for slot in near:
            pl.semaphore_signal(stage, 1, device_id={"slot": slot}, device_id_type=MESH)

    loads = [
        pltpu.make_async_copy(tiles_in.at[:, pl.ds(0, HEAD)], tiles.at[0], small_sem.at[0]),
        pltpu.make_async_copy(tiles_in.at[:, pl.ds(HEAD, HEAD)], tiles.at[1], small_sem.at[4]),
        pltpu.make_async_copy(offset_in, offs, small_sem.at[1]),
        pltpu.make_async_copy(pos_in, pos_v, small_sem.at[2]),
        pltpu.make_async_copy(count_in, count, small_sem.at[5]),
        pltpu.make_async_copy(steps_in, steps_v, small_sem.at[6]),
        pltpu.make_async_copy(freq_in, freq_v, small_sem.at[3]),
    ]
    kv_load = pltpu.make_async_copy(kv_store, kv, load_sem.at[0])
    hid_load = pltpu.make_async_copy(hidden.at[0], hid, load_sem.at[1])
    w_loads = [
        pltpu.make_async_copy(a, b, w_sem.at[n])
        for n, (a, b) in enumerate(((w_query, wq), (key_weight, wk), (value_weight, wv), (w_out, wo)))
    ]
    for copy in loads + [kv_load]:
        copy.start()
    for copy in loads:
        copy.wait()

    lane = lax.broadcasted_iota(i32, (STEPS, HEAD), 1)
    mine_offs = offs[pl.ds(me, 1), :]
    freq = freq_v[...]
    half_sign = jnp.where(lax.broadcasted_iota(i32, (1, HEAD), 1) < HEAD // 2, -1.0, 1.0)
    id_rows = jnp.zeros((STEPS, HEAD), i32)
    for b in range(2):
        block = tiles[b]
        mine = (block >> 7) == me
        code = lane * HEAD + (block & 127)
        picks = (
            jnp.min(jnp.where(mine, code, FAR), axis=1, keepdims=True),
            jnp.max(jnp.where(mine, code, 0), axis=1, keepdims=True),
        )
        for k, pick in enumerate(picks):
            local, tile = pick & 127, pick >> 7
            offset = jnp.sum(jnp.where(lane == local, mine_offs, 0), axis=1, keepdims=True)
            angle = ((b * HEAD + tile) * 8 - offset).astype(f32) * freq
            turn_c[b * 2 + k] = jnp.cos(angle)
            turn_s[b * 2 + k] = jnp.sin(angle) * half_sign
            id_rows = jnp.where(lane == b * 2 + k, local, id_rows)
    ids_v[...] = id_rows
    id_copy = pltpu.make_async_copy(ids_v, ids, ids_sem)
    id_copy.start()
    id_copy.wait()
    kv_load.wait()
    for copy in [hid_load] + w_loads:
        copy.start()

    def pack(step, slot):
        for b in range(2):
            for kind in range(2):
                rows = []
                for k in range(2):
                    rows.append(kv[ids[slot, b * 2 + k], kind].astype(f32))
                for h in range(4):
                    heads = []
                    for k in range(2):
                        u = rows[k][:, h * HEAD : (h + 1) * HEAD]
                        if kind == 0:
                            cosine = turn_c[b * 2 + k, pl.ds(slot, 1), :]
                            sine = turn_s[b * 2 + k, pl.ds(slot, 1), :]
                            u = u * cosine + pltpu.roll(u, HEAD // 2, axis=1) * sine
                        heads.append(u)
                    send[step * 2 + h // 2, kind, b * 16 : (b + 1) * 16, (h % 2) * HEAD : (h % 2 + 1) * HEAD] = (
                        jnp.concatenate(heads, axis=0).astype(bf16)
                    )

    pl.semaphore_wait(barrier, 16)
    tell(second_stage)

    pack(0, s)
    self_copy = pltpu.make_async_copy(send.at[r], recv.at[r], self_sem)
    self_copy.start()
    pair_copy = pltpu.make_async_remote_copy(
        send.at[1 - r], recv.at[r], pair_send, pair_recv, device_id={"row": 1 - r}, device_id_type=MESH
    )
    pair_copy.start()

    def ship(step, dz, dy, dx):
        slot = target(dz, dy, dx)
        pack(step, slot)
        for row in range(2):
            pltpu.make_async_remote_copy(
                send.at[step * 2 + row],
                recv.at[step * 2 + r],
                send_sem,
                recv_sem.at[step // CHUNK],
                device_id={"slot": slot, "row": row},
                device_id_type=MESH,
            ).start()

    def ship_one(j, carry):
        ship(2 * j - 1, j, 0, 0)
        ship(2 * j, 0, j, 0)
        return carry

    def ship_two(j, carry):
        step = 5 * j + 3
        ship(step, j, 0, 1)
        ship(step + 1, 0, j, 1)
        for n in range(3):
            ship(step + 2 + n, j, 1 + (j + n) % 3, 0)
        return carry

    def ship_three(m, carry):
        ship(23 + m, 1 + m // 3, 1 + (m // 3 + m) % 3, 1)
        return carry

    lax.fori_loop(1, 4, ship_one, 0)
    ship(7, 0, 0, 1)
    pl.semaphore_wait(second_stage, 7)
    tell(third_stage)
    lax.fori_loop(1, 4, ship_two, 0)
    pl.semaphore_wait(third_stage, 7)
    lax.fori_loop(0, 9, ship_three, 0)

    hid_load.wait()
    for copy in w_loads[:3]:
        copy.wait()
    x_in = hid[...]

    def project(side, into):
        def body(n, carry):
            cols = pl.ds(pl.multiple_of(side * 1024 + n * 256, 256), 256)
            into[:, pl.ds(pl.multiple_of(n * 256, 256), 256)] = jnp.dot(
                x_in, wq[:, cols], preferred_element_type=f32
            )
            return carry

        lax.fori_loop(0, 4, body, 0)
        cols = pl.ds(pl.multiple_of(side * 256, 256), 256)
        into[:, 1024:1280] = jnp.dot(x_in, wk[:, cols], preferred_element_type=f32)
        into[:, 1280:1536] = jnp.dot(x_in, wv[:, cols], preferred_element_type=f32)

    project(1 - r, part_send)
    part_copy = pltpu.make_async_remote_copy(
        part_send, part_recv, part_ssem, part_rsem, device_id={"row": 1 - r}, device_id_type=MESH
    )
    part_copy.start()
    project(r, part_own)

    def column(row_vector):
        return jnp.transpose(jnp.broadcast_to(row_vector, (HEAD, HEAD)))

    pos_col = column(pos_v[...])
    pos_m[:, :HEAD] = pos_col
    pos_m[:, HEAD:] = pos_col
    owner_cols = [column(tiles[b, pl.ds(s, 1), :] >> 7) for b in range(2)]
    block_of = (lax.broadcasted_iota(i32, (TOK, HEAD), 1) >> 4) & 1
    picked = jnp.where(block_of == 0, owner_cols[0], owner_cols[1])
    owner_sel[:, :HEAD] = picked
    owner_sel[:, HEAD:] = picked
    token_angle = pos_col.astype(f32) * freq
    token_c = jnp.cos(token_angle)
    token_s = jnp.sin(token_angle) * half_sign

    part_copy.wait()

    def total(lo):
        return part_own[:, lo : lo + HEAD] + part_recv[:, lo : lo + HEAD]

    def turned(lo):
        u = total(lo)
        return (u * token_c + pltpu.roll(u, HEAD // 2, axis=1) * token_s).astype(bf16)

    for h in range(8):
        q[h] = turned(h * HEAD)
    for h in range(2):
        k_new[:, h * HEAD : (h + 1) * HEAD] = turned(1024 + h * HEAD)
        v_new[:, h * HEAD : (h + 1) * HEAD] = total(1280 + h * HEAD).astype(bf16)

    def scores(qh, kh, mask):
        sc = lax.dot_general(qh, kh, (((1,), (1,)), ((), ())), preferred_element_type=f32)
        return jnp.where(mask, sc * SCALE, NEG)

    fresh = lax.broadcasted_iota(i32, (TOK, TOK), 1) <= lax.broadcasted_iota(i32, (TOK, TOK), 0)
    for h in range(8):
        g = h // 4
        sc = scores(q[h], k_new[:, g * HEAD : (g + 1) * HEAD], fresh)
        peak = jnp.max(sc, axis=1, keepdims=True)
        p = jnp.exp2(sc - peak)
        m_s[h] = jnp.broadcast_to(peak, (TOK, HEAD))
        l_s[h] = jnp.broadcast_to(jnp.sum(p, axis=1, keepdims=True), (TOK, HEAD))
        acc[h] = jnp.dot(p.astype(bf16), v_new[:, g * HEAD : (g + 1) * HEAD], preferred_element_type=f32)

    limit = count[s] * 8
    lane2 = lax.broadcasted_iota(i32, (1, KEYS), 1)
    src = lane2 >> 5
    in_block, second, unit = (lane2 >> 4) & 1, (lane2 >> 3) & 1, lane2 & 7
    src_row = src & 1
    src_sign = 1 - 2 * src_row
    tile_row = lax.broadcasted_iota(i32, (TOK, KEYS), 0)

    def attend(n, done=None):
        code = steps_v[n : n + 1, :]
        dz, dy, dx = code >> 4, (code >> 2) & 3, code & 1
        source = ((((z - src_sign * dz + 4) & 3) * NY + ((y - src_sign * dy + 4) & 3)) * NX + ((x + dx) & 1)) * 2 + src_row
        here = owner_sel[...] == source
        first = jnp.min(jnp.where(here, tile_row, FAR), axis=0, keepdims=True)
        last = jnp.max(jnp.where(here, tile_row, 0), axis=0, keepdims=True)
        key_pos = (in_block * HEAD + jnp.where(second == 0, first, last)) * 8 + unit
        pos = pos_m[...]
        redone = jnp.max(jnp.where(pos == key_pos, 1, 0), axis=0, keepdims=True)
        key_pos = jnp.where(jnp.logical_or(redone > 0, key_pos >= limit), FAR, key_pos)
        mask = key_pos <= pos
        for g in range(2):
            kh = recv[pl.ds(n * 8, 8), 0, :, g * HEAD : (g + 1) * HEAD].reshape(KEYS, HEAD)
            vh = recv[pl.ds(n * 8, 8), 1, :, g * HEAD : (g + 1) * HEAD].reshape(KEYS, HEAD)
            for j in range(4):
                h = g * 4 + j
                sc = scores(q[h], kh, mask)
                old = m_s[h]
                peak = jnp.maximum(old, jnp.max(sc, axis=1, keepdims=True))
                p = jnp.exp2(sc - jnp.concatenate([peak, peak], axis=1))
                shrink = jnp.exp2(old - peak)
                m_s[h] = peak
                l_s[h] = l_s[h] * shrink + jnp.sum(p, axis=1, keepdims=True)
                acc[h] = acc[h] * shrink + jnp.dot(p.astype(bf16), vh, preferred_element_type=f32)
                if done is not None:
                    done(h)

    def landed(first, many, sem):
        return pltpu.make_async_copy(
            recv.at[pl.ds(first, many)], recv.at[pl.ds(first, many)], sem
        )

    def att_copy(n):
        part = att.at[r]
        return pltpu.make_async_remote_copy(
            part, part, att_ssem.at[n], att_rsem.at[n], device_id={"row": 1 - r}, device_id_type=MESH
        )

    def share(h):
        att[r, :, h * HEAD : (h + 1) * HEAD] = (acc[h] / l_s[h]).astype(bf16)
        if h == 7:
            att_copy(0).start()

    self_copy.wait()
    pair_copy.wait()
    for n in range(CHUNKS):
        if n == 0:
            landed(2, 6, recv_sem.at[0]).wait()
        else:
            landed(8 * n, 8, recv_sem.at[n]).wait()
        attend(n)

    for h in range(8):
        share(h)
    w_loads[3].wait()

    def out_cols(n):
        return pl.ds(pl.multiple_of(n * 256, 256), 256)

    def first_half(n, carry):
        rows = pl.ds(pl.multiple_of(r * 1024, 1024), 1024)
        o_acc[:, out_cols(n)] = jnp.dot(att[r], wo[rows, out_cols(n)], preferred_element_type=f32)
        return carry

    lax.fori_loop(0, 8, first_half, 0)
    att_copy(0).wait()

    def o_copy(n):
        return pltpu.make_async_remote_copy(
            o_send.at[n], o_recv.at[n], o_ssem.at[n], o_rsem.at[n], device_id={"col": 1 - c}, device_id_type=MESH
        )

    def second_half(n, carry):
        rows = pl.ds(pl.multiple_of((1 - r) * 1024, 1024), 1024)
        o_acc[:, out_cols(n)] += jnp.dot(att[1 - r], wo[rows, out_cols(n)], preferred_element_type=f32)
        o_send[n] = o_acc[pl.ds(pl.multiple_of((1 - c) * 64, 64), 64), out_cols(n)].astype(bf16)
        o_copy(n).start()
        return carry

    own_rows = pl.ds(pl.multiple_of(c * 64, 64), 64)
    lax.fori_loop(0, 8, second_half, 0)

    def finish(n, carry):
        o_copy(n).wait()
        out[0, :, out_cols(n)] = (o_acc[own_rows, out_cols(n)] + o_recv[n].astype(f32)).astype(bf16)
        return carry

    lax.fori_loop(0, 8, finish, 0)
    pltpu.make_async_copy(send.at[pl.ds(2, 62)], send.at[pl.ds(2, 62)], send_sem).wait()


def on_device(
    hidden, w_query, key_weight, value_weight, w_out, kv_store,
    stretch_offset, tile_stretch, slot_count, recomp_pos,
):
    freq = (ROPE_BASE ** (-2.0 * np.arange(HEAD // 2, dtype=np.float32) / HEAD)).astype(np.float32)
    freq = jnp.asarray(np.concatenate([freq, freq])[None, :])
    steps = np.repeat([dz * 16 + dy * 4 + dx for dz, dy, dx in send_order()], 2 * MSG).reshape(CHUNKS, KEYS)
    steps = jnp.asarray(steps, i32)
    dma = pltpu.SemaphoreType.DMA
    operands = (
        hidden, w_query, key_weight, value_weight, w_out, kv_store,
        stretch_offset.reshape(64, 128), tile_stretch, slot_count, recomp_pos, freq, steps,
    )
    return pl.pallas_call(
        kernel,
        out_shape=jax.ShapeDtypeStruct((1, 64, 2048), bf16),
        in_specs=[pl.BlockSpec(memory_space=pltpu.HBM)] * 12,
        out_specs=pl.BlockSpec(memory_space=pltpu.VMEM),
        scratch_shapes=[
            pltpu.VMEM((TOK, 2048), bf16),
            pltpu.VMEM((2048, 2048), bf16),
            pltpu.VMEM((2048, 512), bf16),
            pltpu.VMEM((2048, 512), bf16),
            pltpu.VMEM((2048, 2048), bf16),
            pltpu.VMEM((128, 2, 8, 512), bf16),
            pltpu.VMEM((64, 128), i32),
            pltpu.VMEM((2, 32, 128), i32),
            pltpu.SMEM((32,), i32),
            pltpu.VMEM((1, 128), i32),
            pltpu.VMEM((1, 128), f32),
            pltpu.VMEM((CHUNKS, KEYS), i32),
            pltpu.VMEM((2 * STEPS, 2, MSG, 256), bf16),
            pltpu.VMEM((2 * STEPS, 2, MSG, 256), bf16),
            pltpu.VMEM((STEPS, HEAD), i32),
            pltpu.SMEM((STEPS, HEAD), i32),
            pltpu.VMEM((4, STEPS, HEAD), f32),
            pltpu.VMEM((4, STEPS, HEAD), f32),
            pltpu.VMEM((TOK, 1536), f32),
            pltpu.VMEM((TOK, 1536), f32),
            pltpu.VMEM((TOK, 1536), f32),
            pltpu.VMEM((8, TOK, HEAD), bf16),
            pltpu.VMEM((TOK, 256), bf16),
            pltpu.VMEM((TOK, 256), bf16),
            pltpu.VMEM((TOK, KEYS), i32),
            pltpu.VMEM((TOK, KEYS), i32),
            pltpu.VMEM((8, TOK, HEAD), f32),
            pltpu.VMEM((8, TOK, HEAD), f32),
            pltpu.VMEM((8, TOK, HEAD), f32),
            pltpu.VMEM((2, TOK, 1024), bf16),
            pltpu.VMEM((TOK, 2048), f32),
            pltpu.VMEM((8, 64, 256), bf16),
            pltpu.VMEM((8, 64, 256), bf16),
            dma((2,)), dma((7,)), dma(()), dma((4,)), dma(()), dma(()), dma((CHUNKS,)),
            dma(()), dma(()), dma(()), dma(()), dma((4,)), dma((4,)), dma((8,)), dma((8,)),
            pltpu.SemaphoreType.REGULAR, pltpu.SemaphoreType.REGULAR,
        ],
        compiler_params=pltpu.CompilerParams(
            collective_id=0, has_side_effects=True, vmem_limit_bytes=44 << 20
        ),
        name="joined_attention",
    )(*(pltpu.with_memory_space_constraint(a, pltpu.HBM) for a in operands))


def solution(mesh):
    return jax.shard_map(
        on_device,
        mesh=mesh,
        in_specs=(
            P("slot", None, "row"),
            P("row", "col"),
            P("row", "col"),
            P("row", "col"),
            P("col", "row"),
            P(("slot", "row"), None, None, "col"),
            P(),
            P(),
            P(),
            P("slot", None),
        ),
        out_specs=P("slot", "col", "row"),
        check_vma=False,
    )
```

```python
import functools
import math

import jax
import jax.numpy as jnp
import numpy as np
from jax import lax
from jax.experimental import pallas as pl
from jax.experimental.pallas import tpu as pltpu
from jax.sharding import PartitionSpec as P

HEAD = 128
ROPE_BASE = 500000.0
NEG = -1e30
FAR = 1 << 20
MESH = pl.DeviceIdType.MESH
SCALE = math.log2(math.e) / math.sqrt(HEAD)
f32, bf16, i32 = jnp.float32, jnp.bfloat16, jnp.int32

TOK = 128
NZ, NY, NX = 4, 4, 2
STEPS = NZ * NY * NX
CHUNK = 4
CHUNKS = STEPS // CHUNK
MSG = 32
KEYS = CHUNK * 2 * MSG


def send_order():
    order = [(0, 0, 0), (0, 0, 1)]
    for j in range(1, 4):
        order += [(j, 0, 0), (0, j, 0)]
    for j in range(1, 4):
        order += [(j, 0, 1), (0, j, 1)]
    for m in range(9):
        order += [(*far(m), 1), (*flat(m), 0)]
    return order


def far(m):
    return 1 + (m + 1) % 3, 1 + (m // 3 + m + 2) % 3


def flat(m):
    return 1 + m % 3, 1 + (m // 3 + m) % 3


def kernel(
    hidden, w_query, key_weight, value_weight, w_out, kv_store,
    offset_in, tiles_in, count_in, pos_in, freq_in, steps_in,
    out,
    hid, wq, wk, wv, wo, kv, offs, tiles, count, pos_v, freq_v, steps_v,
    send, recv, ids_v, ids, turn_c, turn_s,
    part_send, part_recv, part_own,
    q, k_new, v_new, owner_sel, pos_m,
    m_s, l_s, acc, att, o_acc, o_send, o_recv,
    load_sem, small_sem, ids_sem, w_sem, self_sem, send_sem, recv_sem,
    pair_send, pair_recv, part_ssem, part_rsem, att_ssem, att_rsem, o_ssem, o_rsem, second_stage, third_stage,
):
    s = lax.axis_index("slot")
    r = lax.axis_index("row")
    c = lax.axis_index("col")
    z, y, x = s // (NY * NX), (s // NX) % NY, s % NX
    me = s * 2 + r
    sign = 1 - 2 * r

    def target(dz, dy, dx):
        return ((z + sign * dz + 4) % 4 * NY + (y + sign * dy + 4) % 4) * NX + (x + dx) % 2

    near = [target(j, 0, 0) for j in range(1, 4)] + [target(0, j, 0) for j in range(1, 4)] + [target(0, 0, 1)]

    barrier = pltpu.get_barrier_semaphore()
    pl.semaphore_signal(barrier, 1, device_id={"row": 1 - r}, device_id_type=MESH)
    pl.semaphore_signal(barrier, 1, device_id={"col": 1 - c}, device_id_type=MESH)
    for slot in near:
        for row in range(2):
            pl.semaphore_signal(barrier, 1, device_id={"slot": slot, "row": row}, device_id_type=MESH)

    def tell(stage):
        for slot in near:
            pl.semaphore_signal(stage, 1, device_id={"slot": slot}, device_id_type=MESH)

    loads = [
        pltpu.make_async_copy(tiles_in.at[:, pl.ds(0, HEAD)], tiles.at[0], small_sem.at[0]),
        pltpu.make_async_copy(tiles_in.at[:, pl.ds(HEAD, HEAD)], tiles.at[1], small_sem.at[4]),
        pltpu.make_async_copy(offset_in, offs, small_sem.at[1]),
        pltpu.make_async_copy(pos_in, pos_v, small_sem.at[2]),
        pltpu.make_async_copy(count_in, count, small_sem.at[5]),
        pltpu.make_async_copy(steps_in, steps_v, small_sem.at[6]),
        pltpu.make_async_copy(freq_in, freq_v, small_sem.at[3]),
    ]
    kv_load = pltpu.make_async_copy(kv_store, kv, load_sem.at[0])
    hid_load = pltpu.make_async_copy(hidden.at[0], hid, load_sem.at[1])
    w_loads = [
        pltpu.make_async_copy(a, b, w_sem.at[n])
        for n, (a, b) in enumerate(((w_query, wq), (key_weight, wk), (value_weight, wv), (w_out, wo)))
    ]
    for copy in loads + [kv_load]:
        copy.start()
    for copy in loads:
        copy.wait()

    lane = lax.broadcasted_iota(i32, (STEPS, HEAD), 1)
    mine_offs = offs[pl.ds(me, 1), :]
    freq = freq_v[...]
    half_sign = jnp.where(lax.broadcasted_iota(i32, (1, HEAD), 1) < HEAD // 2, -1.0, 1.0)
    id_rows = jnp.zeros((STEPS, HEAD), i32)
    for b in range(2):
        block = tiles[b]
        mine = (block >> 7) == me
        code = lane * HEAD + (block & 127)
        picks = (
            jnp.min(jnp.where(mine, code, FAR), axis=1, keepdims=True),
            jnp.max(jnp.where(mine, code, 0), axis=1, keepdims=True),
        )
        for k, pick in enumerate(picks):
            local, tile = pick & 127, pick >> 7
            offset = jnp.sum(jnp.where(lane == local, mine_offs, 0), axis=1, keepdims=True)
            angle = ((b * HEAD + tile) * 8 - offset).astype(f32) * freq
            turn_c[b * 2 + k] = jnp.cos(angle)
            turn_s[b * 2 + k] = jnp.sin(angle) * half_sign
            id_rows = jnp.where(lane == b * 2 + k, local, id_rows)
    ids_v[...] = id_rows
    id_copy = pltpu.make_async_copy(ids_v, ids, ids_sem)
    id_copy.start()
    id_copy.wait()
    kv_load.wait()
    for copy in [hid_load] + w_loads:
        copy.start()

    def pack(step, slot):
        for b in range(2):
            for kind in range(2):
                rows = []
                for k in range(2):
                    rows.append(kv[ids[slot, b * 2 + k], kind].astype(f32))
                for h in range(4):
                    heads = []
                    for k in range(2):
                        u = rows[k][:, h * HEAD : (h + 1) * HEAD]
                        if kind == 0:
                            cosine = turn_c[b * 2 + k, pl.ds(slot, 1), :]
                            sine = turn_s[b * 2 + k, pl.ds(slot, 1), :]
                            u = u * cosine + pltpu.roll(u, HEAD // 2, axis=1) * sine
                        heads.append(u)
                    send[step * 2 + h // 2, kind, b * 16 : (b + 1) * 16, (h % 2) * HEAD : (h % 2 + 1) * HEAD] = (
                        jnp.concatenate(heads, axis=0).astype(bf16)
                    )

    pl.semaphore_wait(barrier, 16)
    tell(second_stage)

    pack(0, s)
    self_copy = pltpu.make_async_copy(send.at[r], recv.at[r], self_sem)
    self_copy.start()
    pair_copy = pltpu.make_async_remote_copy(
        send.at[1 - r], recv.at[r], pair_send, pair_recv, device_id={"row": 1 - r}, device_id_type=MESH
    )
    pair_copy.start()

    def ship(step, dz, dy, dx):
        slot = target(dz, dy, dx)
        pack(step, slot)
        for row in range(2):
            pltpu.make_async_remote_copy(
                send.at[step * 2 + row],
                recv.at[step * 2 + r],
                send_sem,
                recv_sem.at[step // CHUNK],
                device_id={"slot": slot, "row": row},
                device_id_type=MESH,
            ).start()

    def ship_one(j, carry):
        ship(2 * j, j, 0, 0)
        ship(2 * j + 1, 0, j, 0)
        return carry

    def ship_two(j, carry):
        ship(2 * j + 6, j, 0, 1)
        ship(2 * j + 7, 0, j, 1)
        return carry

    def ship_rest(m, carry):
        ship(2 * m + 14, *far(m), 1)
        ship(2 * m + 15, *flat(m), 0)
        return carry

    ship(1, 0, 0, 1)
    lax.fori_loop(1, 4, ship_one, 0)
    pl.semaphore_wait(second_stage, 7)
    tell(third_stage)
    lax.fori_loop(1, 4, ship_two, 0)
    pl.semaphore_wait(third_stage, 7)
    lax.fori_loop(0, 9, ship_rest, 0)

    hid_load.wait()
    for copy in w_loads[:3]:
        copy.wait()
    x_in = hid[...]

    def project(side, into):
        def body(n, carry):
            cols = pl.ds(pl.multiple_of(side * 1024 + n * 256, 256), 256)
            into[:, pl.ds(pl.multiple_of(n * 256, 256), 256)] = jnp.dot(
                x_in, wq[:, cols], preferred_element_type=f32
            )
            return carry

        lax.fori_loop(0, 4, body, 0)
        cols = pl.ds(pl.multiple_of(side * 256, 256), 256)
        into[:, 1024:1280] = jnp.dot(x_in, wk[:, cols], preferred_element_type=f32)
        into[:, 1280:1536] = jnp.dot(x_in, wv[:, cols], preferred_element_type=f32)

    project(1 - r, part_send)
    part_copy = pltpu.make_async_remote_copy(
        part_send, part_recv, part_ssem, part_rsem, device_id={"row": 1 - r}, device_id_type=MESH
    )
    part_copy.start()
    project(r, part_own)

    def column(row_vector):
        return jnp.transpose(jnp.broadcast_to(row_vector, (HEAD, HEAD)))

    pos_col = column(pos_v[...])
    pos_m[:, :HEAD] = pos_col
    pos_m[:, HEAD:] = pos_col
    owner_cols = [column(tiles[b, pl.ds(s, 1), :] >> 7) for b in range(2)]
    block_of = (lax.broadcasted_iota(i32, (TOK, HEAD), 1) >> 4) & 1
    picked = jnp.where(block_of == 0, owner_cols[0], owner_cols[1])
    owner_sel[:, :HEAD] = picked
    owner_sel[:, HEAD:] = picked
    token_angle = pos_col.astype(f32) * freq
    token_c = jnp.cos(token_angle)
    token_s = jnp.sin(token_angle) * half_sign

    part_copy.wait()

    def total(lo):
        return part_own[:, lo : lo + HEAD] + part_recv[:, lo : lo + HEAD]

    def turned(lo):
        u = total(lo)
        return (u * token_c + pltpu.roll(u, HEAD // 2, axis=1) * token_s).astype(bf16)

    for h in range(8):
        q[h] = turned(h * HEAD)
    for h in range(2):
        k_new[:, h * HEAD : (h + 1) * HEAD] = turned(1024 + h * HEAD)
        v_new[:, h * HEAD : (h + 1) * HEAD] = total(1280 + h * HEAD).astype(bf16)

    def scores(qh, kh, mask):
        sc = lax.dot_general(qh, kh, (((1,), (1,)), ((), ())), preferred_element_type=f32)
        return jnp.where(mask, sc * SCALE, NEG)

    fresh = lax.broadcasted_iota(i32, (TOK, TOK), 1) <= lax.broadcasted_iota(i32, (TOK, TOK), 0)
    for h in range(8):
        g = h // 4
        sc = scores(q[h], k_new[:, g * HEAD : (g + 1) * HEAD], fresh)
        peak = jnp.max(sc, axis=1, keepdims=True)
        p = jnp.exp2(sc - peak)
        m_s[h] = jnp.broadcast_to(peak, (TOK, HEAD))
        l_s[h] = jnp.broadcast_to(jnp.sum(p, axis=1, keepdims=True), (TOK, HEAD))
        acc[h] = jnp.dot(p.astype(bf16), v_new[:, g * HEAD : (g + 1) * HEAD], preferred_element_type=f32)

    limit = count[s] * 8
    lane2 = lax.broadcasted_iota(i32, (1, KEYS), 1)
    src = lane2 >> 5
    in_block, second, unit = (lane2 >> 4) & 1, (lane2 >> 3) & 1, lane2 & 7
    src_row = src & 1
    src_sign = 1 - 2 * src_row
    tile_row = lax.broadcasted_iota(i32, (TOK, KEYS), 0)

    def attend(n, done=None):
        code = steps_v[n : n + 1, :]
        dz, dy, dx = code >> 4, (code >> 2) & 3, code & 1
        source = ((((z - src_sign * dz + 4) & 3) * NY + ((y - src_sign * dy + 4) & 3)) * NX + ((x + dx) & 1)) * 2 + src_row
        here = owner_sel[...] == source
        first = jnp.min(jnp.where(here, tile_row, FAR), axis=0, keepdims=True)
        last = jnp.max(jnp.where(here, tile_row, 0), axis=0, keepdims=True)
        key_pos = (in_block * HEAD + jnp.where(second == 0, first, last)) * 8 + unit
        pos = pos_m[...]
        redone = jnp.max(jnp.where(pos == key_pos, 1, 0), axis=0, keepdims=True)
        key_pos = jnp.where(jnp.logical_or(redone > 0, key_pos >= limit), FAR, key_pos)
        mask = key_pos <= pos
        for g in range(2):
            kh = recv[pl.ds(n * 8, 8), 0, :, g * HEAD : (g + 1) * HEAD].reshape(KEYS, HEAD)
            vh = recv[pl.ds(n * 8, 8), 1, :, g * HEAD : (g + 1) * HEAD].reshape(KEYS, HEAD)
            for j in range(4):
                h = g * 4 + j
                sc = scores(q[h], kh, mask)
                old = m_s[h]
                peak = jnp.maximum(old, jnp.max(sc, axis=1, keepdims=True))
                p = jnp.exp2(sc - jnp.concatenate([peak, peak], axis=1))
                shrink = jnp.exp2(old - peak)
                m_s[h] = peak
                l_s[h] = l_s[h] * shrink + jnp.sum(p, axis=1, keepdims=True)
                acc[h] = acc[h] * shrink + jnp.dot(p.astype(bf16), vh, preferred_element_type=f32)
                if done is not None:
                    done(h)

    def landed(first, many, sem):
        return pltpu.make_async_copy(
            recv.at[pl.ds(first, many)], recv.at[pl.ds(first, many)], sem
        )

    def att_copy(n):
        part = att.at[r]
        return pltpu.make_async_remote_copy(
            part, part, att_ssem.at[n], att_rsem.at[n], device_id={"row": 1 - r}, device_id_type=MESH
        )

    def share(h):
        att[r, :, h * HEAD : (h + 1) * HEAD] = (acc[h] / l_s[h]).astype(bf16)
        if h == 7:
            att_copy(0).start()

    self_copy.wait()
    pair_copy.wait()
    for n in range(CHUNKS):
        if n == 0:
            landed(2, 6, recv_sem.at[0]).wait()
        else:
            landed(8 * n, 8, recv_sem.at[n]).wait()
        attend(n)

    for h in range(8):
        share(h)
    w_loads[3].wait()

    def out_cols(n):
        return pl.ds(pl.multiple_of(n * 256, 256), 256)

    def first_half(n, carry):
        rows = pl.ds(pl.multiple_of(r * 1024, 1024), 1024)
        o_acc[:, out_cols(n)] = jnp.dot(att[r], wo[rows, out_cols(n)], preferred_element_type=f32)
        return carry

    lax.fori_loop(0, 8, first_half, 0)
    att_copy(0).wait()

    def o_copy(n):
        return pltpu.make_async_remote_copy(
            o_send.at[n], o_recv.at[n], o_ssem.at[n], o_rsem.at[n], device_id={"col": 1 - c}, device_id_type=MESH
        )

    def second_half(n, carry):
        rows = pl.ds(pl.multiple_of((1 - r) * 1024, 1024), 1024)
        o_acc[:, out_cols(n)] += jnp.dot(att[1 - r], wo[rows, out_cols(n)], preferred_element_type=f32)
        o_send[n] = o_acc[pl.ds(pl.multiple_of((1 - c) * 64, 64), 64), out_cols(n)].astype(bf16)
        o_copy(n).start()
        return carry

    own_rows = pl.ds(pl.multiple_of(c * 64, 64), 64)
    lax.fori_loop(0, 8, second_half, 0)

    def finish(n, carry):
        o_copy(n).wait()
        out[0, :, out_cols(n)] = (o_acc[own_rows, out_cols(n)] + o_recv[n].astype(f32)).astype(bf16)
        return carry

    lax.fori_loop(0, 8, finish, 0)
    pltpu.make_async_copy(send.at[pl.ds(2, 62)], send.at[pl.ds(2, 62)], send_sem).wait()


def on_device(
    hidden, w_query, key_weight, value_weight, w_out, kv_store,
    stretch_offset, tile_stretch, slot_count, recomp_pos,
):
    freq = (ROPE_BASE ** (-2.0 * np.arange(HEAD // 2, dtype=np.float32) / HEAD)).astype(np.float32)
    freq = jnp.asarray(np.concatenate([freq, freq])[None, :])
    steps = np.repeat([dz * 16 + dy * 4 + dx for dz, dy, dx in send_order()], 2 * MSG).reshape(CHUNKS, KEYS)
    steps = jnp.asarray(steps, i32)
    dma = pltpu.SemaphoreType.DMA
    operands = (
        hidden, w_query, key_weight, value_weight, w_out, kv_store,
        stretch_offset.reshape(64, 128), tile_stretch, slot_count, recomp_pos, freq, steps,
    )
    return pl.pallas_call(
        kernel,
        out_shape=jax.ShapeDtypeStruct((1, 64, 2048), bf16),
        in_specs=[pl.BlockSpec(memory_space=pltpu.HBM)] * 12,
        out_specs=pl.BlockSpec(memory_space=pltpu.VMEM),
        scratch_shapes=[
            pltpu.VMEM((TOK, 2048), bf16),
            pltpu.VMEM((2048, 2048), bf16),
            pltpu.VMEM((2048, 512), bf16),
            pltpu.VMEM((2048, 512), bf16),
            pltpu.VMEM((2048, 2048), bf16),
            pltpu.VMEM((128, 2, 8, 512), bf16),
            pltpu.VMEM((64, 128), i32),
            pltpu.VMEM((2, 32, 128), i32),
            pltpu.SMEM((32,), i32),
            pltpu.VMEM((1, 128), i32),
            pltpu.VMEM((1, 128), f32),
            pltpu.VMEM((CHUNKS, KEYS), i32),
            pltpu.VMEM((2 * STEPS, 2, MSG, 256), bf16),
            pltpu.VMEM((2 * STEPS, 2, MSG, 256), bf16),
            pltpu.VMEM((STEPS, HEAD), i32),
            pltpu.SMEM((STEPS, HEAD), i32),
            pltpu.VMEM((4, STEPS, HEAD), f32),
            pltpu.VMEM((4, STEPS, HEAD), f32),
            pltpu.VMEM((TOK, 1536), f32),
            pltpu.VMEM((TOK, 1536), f32),
            pltpu.VMEM((TOK, 1536), f32),
            pltpu.VMEM((8, TOK, HEAD), bf16),
            pltpu.VMEM((TOK, 256), bf16),
            pltpu.VMEM((TOK, 256), bf16),
            pltpu.VMEM((TOK, KEYS), i32),
            pltpu.VMEM((TOK, KEYS), i32),
            pltpu.VMEM((8, TOK, HEAD), f32),
            pltpu.VMEM((8, TOK, HEAD), f32),
            pltpu.VMEM((8, TOK, HEAD), f32),
            pltpu.VMEM((2, TOK, 1024), bf16),
            pltpu.VMEM((TOK, 2048), f32),
            pltpu.VMEM((8, 64, 256), bf16),
            pltpu.VMEM((8, 64, 256), bf16),
            dma((2,)), dma((7,)), dma(()), dma((4,)), dma(()), dma(()), dma((CHUNKS,)),
            dma(()), dma(()), dma(()), dma(()), dma((4,)), dma((4,)), dma((8,)), dma((8,)),
            pltpu.SemaphoreType.REGULAR, pltpu.SemaphoreType.REGULAR,
        ],
        compiler_params=pltpu.CompilerParams(
            collective_id=0, has_side_effects=True, vmem_limit_bytes=44 << 20
        ),
        name="joined_attention",
    )(*(pltpu.with_memory_space_constraint(a, pltpu.HBM) for a in operands))


def solution(mesh):
    return jax.shard_map(
        on_device,
        mesh=mesh,
        in_specs=(
            P("slot", None, "row"),
            P("row", "col"),
            P("row", "col"),
            P("row", "col"),
            P("col", "row"),
            P(("slot", "row"), None, None, "col"),
            P(),
            P(),
            P(),
            P("slot", None),
        ),
        out_specs=P("slot", "col", "row"),
        check_vma=False,
    )
```

```python
import functools
import math

import jax
import jax.numpy as jnp
import numpy as np
from jax import lax
from jax.experimental import pallas as pl
from jax.experimental.pallas import tpu as pltpu
from jax.sharding import PartitionSpec as P

HEAD = 128
ROPE_BASE = 500000.0
NEG = -1e30
FAR = 1 << 20
MESH = pl.DeviceIdType.MESH
SCALE = math.log2(math.e) / math.sqrt(HEAD)
f32, bf16, i32 = jnp.float32, jnp.bfloat16, jnp.int32

TOK = 128
NZ, NY, NX = 4, 4, 2
STEPS = NZ * NY * NX
CHUNK = 4
CHUNKS = STEPS // CHUNK
MSG = 32
KEYS = CHUNK * 2 * MSG


def send_order():
    order = [(0, 0, 0), (0, 0, 1)]
    for j in range(1, 4):
        order += [(j, 0, 0), (0, j, 0)]
    for j in range(1, 4):
        order += [(j, 0, 1), (0, j, 1)]
    for m in range(9):
        order += [(*far(m), 1), (*flat(m), 0)]
    return order


def far(m):
    return 1 + (2 * m + 1) % 3, 1 + (m // 3 + m + 2) % 3


def flat(m):
    return 1 + m % 3, 1 + (m // 3 + m) % 3


def kernel(
    hidden, w_query, key_weight, value_weight, w_out, kv_store,
    offset_in, tiles_in, count_in, pos_in, freq_in, steps_in,
    out,
    hid, wq, wk, wv, wo, kv, offs, tiles, count, pos_v, freq_v, steps_v,
    send, recv, ids_v, ids, turn_c, turn_s,
    part_send, part_recv, part_own,
    q, k_new, v_new, owner_sel, pos_m,
    m_s, l_s, acc, att, o_acc, o_send, o_recv,
    load_sem, small_sem, ids_sem, w_sem, self_sem, send_sem, recv_sem,
    pair_send, pair_recv, part_ssem, part_rsem, att_ssem, att_rsem, o_ssem, o_rsem, second_stage, third_stage,
):
    s = lax.axis_index("slot")
    r = lax.axis_index("row")
    c = lax.axis_index("col")
    z, y, x = s // (NY * NX), (s // NX) % NY, s % NX
    me = s * 2 + r
    sign = 1 - 2 * r

    def target(dz, dy, dx):
        return ((z + sign * dz + 4) % 4 * NY + (y + sign * dy + 4) % 4) * NX + (x + dx) % 2

    near = [target(j, 0, 0) for j in range(1, 4)] + [target(0, j, 0) for j in range(1, 4)] + [target(0, 0, 1)]

    barrier = pltpu.get_barrier_semaphore()
    pl.semaphore_signal(barrier, 1, device_id={"row": 1 - r}, device_id_type=MESH)
    pl.semaphore_signal(barrier, 1, device_id={"col": 1 - c}, device_id_type=MESH)
    for slot in near:
        for row in range(2):
            pl.semaphore_signal(barrier, 1, device_id={"slot": slot, "row": row}, device_id_type=MESH)

    def tell(stage):
        for slot in near:
            pl.semaphore_signal(stage, 1, device_id={"slot": slot}, device_id_type=MESH)

    loads = [
        pltpu.make_async_copy(tiles_in.at[:, pl.ds(0, HEAD)], tiles.at[0], small_sem.at[0]),
        pltpu.make_async_copy(tiles_in.at[:, pl.ds(HEAD, HEAD)], tiles.at[1], small_sem.at[4]),
        pltpu.make_async_copy(offset_in, offs, small_sem.at[1]),
        pltpu.make_async_copy(pos_in, pos_v, small_sem.at[2]),
        pltpu.make_async_copy(count_in, count, small_sem.at[5]),
        pltpu.make_async_copy(steps_in, steps_v, small_sem.at[6]),
        pltpu.make_async_copy(freq_in, freq_v, small_sem.at[3]),
    ]
    kv_load = pltpu.make_async_copy(kv_store, kv, load_sem.at[0])
    hid_load = pltpu.make_async_copy(hidden.at[0], hid, load_sem.at[1])
    w_loads = [
        pltpu.make_async_copy(a, b, w_sem.at[n])
        for n, (a, b) in enumerate(((w_query, wq), (key_weight, wk), (value_weight, wv), (w_out, wo)))
    ]
    for copy in loads + [kv_load]:
        copy.start()
    for copy in loads:
        copy.wait()

    lane = lax.broadcasted_iota(i32, (STEPS, HEAD), 1)
    mine_offs = offs[pl.ds(me, 1), :]
    freq = freq_v[...]
    half_sign = jnp.where(lax.broadcasted_iota(i32, (1, HEAD), 1) < HEAD // 2, -1.0, 1.0)
    id_rows = jnp.zeros((STEPS, HEAD), i32)
    for b in range(2):
        block = tiles[b]
        mine = (block >> 7) == me
        code = lane * HEAD + (block & 127)
        picks = (
            jnp.min(jnp.where(mine, code, FAR), axis=1, keepdims=True),
            jnp.max(jnp.where(mine, code, 0), axis=1, keepdims=True),
        )
        for k, pick in enumerate(picks):
            local, tile = pick & 127, pick >> 7
            offset = jnp.sum(jnp.where(lane == local, mine_offs, 0), axis=1, keepdims=True)
            angle = ((b * HEAD + tile) * 8 - offset).astype(f32) * freq
            turn_c[b * 2 + k] = jnp.cos(angle)
            turn_s[b * 2 + k] = jnp.sin(angle) * half_sign
            id_rows = jnp.where(lane == b * 2 + k, local, id_rows)
    ids_v[...] = id_rows
    id_copy = pltpu.make_async_copy(ids_v, ids, ids_sem)
    id_copy.start()
    id_copy.wait()
    kv_load.wait()
    for copy in [hid_load] + w_loads:
        copy.start()

    def pack(step, slot):
        for b in range(2):
            for kind in range(2):
                rows = []
                for k in range(2):
                    rows.append(kv[ids[slot, b * 2 + k], kind].astype(f32))
                for h in range(4):
                    heads = []
                    for k in range(2):
                        u = rows[k][:, h * HEAD : (h + 1) * HEAD]
                        if kind == 0:
                            cosine = turn_c[b * 2 + k, pl.ds(slot, 1), :]
                            sine = turn_s[b * 2 + k, pl.ds(slot, 1), :]
                            u = u * cosine + pltpu.roll(u, HEAD // 2, axis=1) * sine
                        heads.append(u)
                    send[step * 2 + h // 2, kind, b * 16 : (b + 1) * 16, (h % 2) * HEAD : (h % 2 + 1) * HEAD] = (
                        jnp.concatenate(heads, axis=0).astype(bf16)
                    )

    pl.semaphore_wait(barrier, 16)
    tell(second_stage)

    pack(0, s)
    self_copy = pltpu.make_async_copy(send.at[r], recv.at[r], self_sem)
    self_copy.start()
    pair_copy = pltpu.make_async_remote_copy(
        send.at[1 - r], recv.at[r], pair_send, pair_recv, device_id={"row": 1 - r}, device_id_type=MESH
    )
    pair_copy.start()

    def ship(step, dz, dy, dx):
        slot = target(dz, dy, dx)
        pack(step, slot)
        for row in range(2):
            pltpu.make_async_remote_copy(
                send.at[step * 2 + row],
                recv.at[step * 2 + r],
                send_sem,
                recv_sem.at[step // CHUNK],
                device_id={"slot": slot, "row": row},
                device_id_type=MESH,
            ).start()

    def ship_one(j, carry):
        ship(2 * j, j, 0, 0)
        ship(2 * j + 1, 0, j, 0)
        return carry

    def ship_two(j, carry):
        ship(2 * j + 6, j, 0, 1)
        ship(2 * j + 7, 0, j, 1)
        return carry

    def ship_rest(m, carry):
        ship(2 * m + 14, *far(m), 1)
        ship(2 * m + 15, *flat(m), 0)
        return carry

    ship(1, 0, 0, 1)
    lax.fori_loop(1, 4, ship_one, 0)
    pl.semaphore_wait(second_stage, 7)
    tell(third_stage)
    lax.fori_loop(1, 4, ship_two, 0)
    pl.semaphore_wait(third_stage, 7)
    lax.fori_loop(0, 9, ship_rest, 0)

    hid_load.wait()
    for copy in w_loads[:3]:
        copy.wait()
    x_in = hid[...]

    def project(side, into):
        def body(n, carry):
            cols = pl.ds(pl.multiple_of(side * 1024 + n * 256, 256), 256)
            into[:, pl.ds(pl.multiple_of(n * 256, 256), 256)] = jnp.dot(
                x_in, wq[:, cols], preferred_element_type=f32
            )
            return carry

        lax.fori_loop(0, 4, body, 0)
        cols = pl.ds(pl.multiple_of(side * 256, 256), 256)
        into[:, 1024:1280] = jnp.dot(x_in, wk[:, cols], preferred_element_type=f32)
        into[:, 1280:1536] = jnp.dot(x_in, wv[:, cols], preferred_element_type=f32)

    project(1 - r, part_send)
    part_copy = pltpu.make_async_remote_copy(
        part_send, part_recv, part_ssem, part_rsem, device_id={"row": 1 - r}, device_id_type=MESH
    )
    part_copy.start()
    project(r, part_own)

    def column(row_vector):
        return jnp.transpose(jnp.broadcast_to(row_vector, (HEAD, HEAD)))

    pos_col = column(pos_v[...])
    pos_m[:, :HEAD] = pos_col
    pos_m[:, HEAD:] = pos_col
    owner_cols = [column(tiles[b, pl.ds(s, 1), :] >> 7) for b in range(2)]
    block_of = (lax.broadcasted_iota(i32, (TOK, HEAD), 1) >> 4) & 1
    picked = jnp.where(block_of == 0, owner_cols[0], owner_cols[1])
    owner_sel[:, :HEAD] = picked
    owner_sel[:, HEAD:] = picked
    token_angle = pos_col.astype(f32) * freq
    token_c = jnp.cos(token_angle)
    token_s = jnp.sin(token_angle) * half_sign

    part_copy.wait()

    def total(lo):
        return part_own[:, lo : lo + HEAD] + part_recv[:, lo : lo + HEAD]

    def turned(lo):
        u = total(lo)
        return (u * token_c + pltpu.roll(u, HEAD // 2, axis=1) * token_s).astype(bf16)

    for h in range(8):
        q[h] = turned(h * HEAD)
    for h in range(2):
        k_new[:, h * HEAD : (h + 1) * HEAD] = turned(1024 + h * HEAD)
        v_new[:, h * HEAD : (h + 1) * HEAD] = total(1280 + h * HEAD).astype(bf16)

    def scores(qh, kh, mask):
        sc = lax.dot_general(qh, kh, (((1,), (1,)), ((), ())), preferred_element_type=f32)
        return jnp.where(mask, sc * SCALE, NEG)

    fresh = lax.broadcasted_iota(i32, (TOK, TOK), 1) <= lax.broadcasted_iota(i32, (TOK, TOK), 0)
    for h in range(8):
        g = h // 4
        sc = scores(q[h], k_new[:, g * HEAD : (g + 1) * HEAD], fresh)
        peak = jnp.max(sc, axis=1, keepdims=True)
        p = jnp.exp2(sc - peak)
        m_s[h] = jnp.broadcast_to(peak, (TOK, HEAD))
        l_s[h] = jnp.broadcast_to(jnp.sum(p, axis=1, keepdims=True), (TOK, HEAD))
        acc[h] = jnp.dot(p.astype(bf16), v_new[:, g * HEAD : (g + 1) * HEAD], preferred_element_type=f32)

    limit = count[s] * 8
    lane2 = lax.broadcasted_iota(i32, (1, KEYS), 1)
    src = lane2 >> 5
    in_block, second, unit = (lane2 >> 4) & 1, (lane2 >> 3) & 1, lane2 & 7
    src_row = src & 1
    src_sign = 1 - 2 * src_row
    tile_row = lax.broadcasted_iota(i32, (TOK, KEYS), 0)

    def attend(n, done=None):
        code = steps_v[n : n + 1, :]
        dz, dy, dx = code >> 4, (code >> 2) & 3, code & 1
        source = ((((z - src_sign * dz + 4) & 3) * NY + ((y - src_sign * dy + 4) & 3)) * NX + ((x + dx) & 1)) * 2 + src_row
        here = owner_sel[...] == source
        first = jnp.min(jnp.where(here, tile_row, FAR), axis=0, keepdims=True)
        last = jnp.max(jnp.where(here, tile_row, 0), axis=0, keepdims=True)
        key_pos = (in_block * HEAD + jnp.where(second == 0, first, last)) * 8 + unit
        pos = pos_m[...]
        redone = jnp.max(jnp.where(pos == key_pos, 1, 0), axis=0, keepdims=True)
        key_pos = jnp.where(jnp.logical_or(redone > 0, key_pos >= limit), FAR, key_pos)
        mask = key_pos <= pos
        for g in range(2):
            kh = recv[pl.ds(n * 8, 8), 0, :, g * HEAD : (g + 1) * HEAD].reshape(KEYS, HEAD)
            vh = recv[pl.ds(n * 8, 8), 1, :, g * HEAD : (g + 1) * HEAD].reshape(KEYS, HEAD)
            for j in range(4):
                h = g * 4 + j
                sc = scores(q[h], kh, mask)
                old = m_s[h]
                peak = jnp.maximum(old, jnp.max(sc, axis=1, keepdims=True))
                p = jnp.exp2(sc - jnp.concatenate([peak, peak], axis=1))
                shrink = jnp.exp2(old - peak)
                m_s[h] = peak
                l_s[h] = l_s[h] * shrink + jnp.sum(p, axis=1, keepdims=True)
                acc[h] = acc[h] * shrink + jnp.dot(p.astype(bf16), vh, preferred_element_type=f32)
                if done is not None:
                    done(h)

    def landed(first, many, sem):
        return pltpu.make_async_copy(
            recv.at[pl.ds(first, many)], recv.at[pl.ds(first, many)], sem
        )

    def att_copy(n):
        part = att.at[r]
        return pltpu.make_async_remote_copy(
            part, part, att_ssem.at[n], att_rsem.at[n], device_id={"row": 1 - r}, device_id_type=MESH
        )

    def share(h):
        att[r, :, h * HEAD : (h + 1) * HEAD] = (acc[h] / l_s[h]).astype(bf16)
        if h == 7:
            att_copy(0).start()

    self_copy.wait()
    pair_copy.wait()
    for n in range(CHUNKS):
        if n == 0:
            landed(2, 6, recv_sem.at[0]).wait()
        else:
            landed(8 * n, 8, recv_sem.at[n]).wait()
        attend(n)

    for h in range(8):
        share(h)
    w_loads[3].wait()

    def out_cols(n):
        return pl.ds(pl.multiple_of(n * 256, 256), 256)

    att_copy(0).wait()

    def o_copy(n):
        return pltpu.make_async_remote_copy(
            o_send.at[n], o_recv.at[n], o_ssem.at[n], o_rsem.at[n], device_id={"col": 1 - c}, device_id_type=MESH
        )

    def out_project(n, carry):
        o_acc[:, out_cols(n)] = jnp.dot(att[0], wo[:1024, out_cols(n)], preferred_element_type=f32) + jnp.dot(
            att[1], wo[1024:, out_cols(n)], preferred_element_type=f32
        )
        o_send[n] = o_acc[pl.ds(pl.multiple_of((1 - c) * 64, 64), 64), out_cols(n)].astype(bf16)
        o_copy(n).start()
        return carry

    own_rows = pl.ds(pl.multiple_of(c * 64, 64), 64)
    lax.fori_loop(0, 8, out_project, 0)

    def finish(n, carry):
        o_copy(n).wait()
        out[0, :, out_cols(n)] = (o_acc[own_rows, out_cols(n)] + o_recv[n].astype(f32)).astype(bf16)
        return carry

    lax.fori_loop(0, 8, finish, 0)
    pltpu.make_async_copy(send.at[pl.ds(2, 62)], send.at[pl.ds(2, 62)], send_sem).wait()


def on_device(
    hidden, w_query, key_weight, value_weight, w_out, kv_store,
    stretch_offset, tile_stretch, slot_count, recomp_pos,
):
    freq = (ROPE_BASE ** (-2.0 * np.arange(HEAD // 2, dtype=np.float32) / HEAD)).astype(np.float32)
    freq = jnp.asarray(np.concatenate([freq, freq])[None, :])
    steps = np.repeat([dz * 16 + dy * 4 + dx for dz, dy, dx in send_order()], 2 * MSG).reshape(CHUNKS, KEYS)
    steps = jnp.asarray(steps, i32)
    dma = pltpu.SemaphoreType.DMA
    operands = (
        hidden, w_query, key_weight, value_weight, w_out, kv_store,
        stretch_offset.reshape(64, 128), tile_stretch, slot_count, recomp_pos, freq, steps,
    )
    return pl.pallas_call(
        kernel,
        out_shape=jax.ShapeDtypeStruct((1, 64, 2048), bf16),
        in_specs=[pl.BlockSpec(memory_space=pltpu.HBM)] * 12,
        out_specs=pl.BlockSpec(memory_space=pltpu.VMEM),
        scratch_shapes=[
            pltpu.VMEM((TOK, 2048), bf16),
            pltpu.VMEM((2048, 2048), bf16),
            pltpu.VMEM((2048, 512), bf16),
            pltpu.VMEM((2048, 512), bf16),
            pltpu.VMEM((2048, 2048), bf16),
            pltpu.VMEM((128, 2, 8, 512), bf16),
            pltpu.VMEM((64, 128), i32),
            pltpu.VMEM((2, 32, 128), i32),
            pltpu.SMEM((32,), i32),
            pltpu.VMEM((1, 128), i32),
            pltpu.VMEM((1, 128), f32),
            pltpu.VMEM((CHUNKS, KEYS), i32),
            pltpu.VMEM((2 * STEPS, 2, MSG, 256), bf16),
            pltpu.VMEM((2 * STEPS, 2, MSG, 256), bf16),
            pltpu.VMEM((STEPS, HEAD), i32),
            pltpu.SMEM((STEPS, HEAD), i32),
            pltpu.VMEM((4, STEPS, HEAD), f32),
            pltpu.VMEM((4, STEPS, HEAD), f32),
            pltpu.VMEM((TOK, 1536), f32),
            pltpu.VMEM((TOK, 1536), f32),
            pltpu.VMEM((TOK, 1536), f32),
            pltpu.VMEM((8, TOK, HEAD), bf16),
            pltpu.VMEM((TOK, 256), bf16),
            pltpu.VMEM((TOK, 256), bf16),
            pltpu.VMEM((TOK, KEYS), i32),
            pltpu.VMEM((TOK, KEYS), i32),
            pltpu.VMEM((8, TOK, HEAD), f32),
            pltpu.VMEM((8, TOK, HEAD), f32),
            pltpu.VMEM((8, TOK, HEAD), f32),
            pltpu.VMEM((2, TOK, 1024), bf16),
            pltpu.VMEM((TOK, 2048), f32),
            pltpu.VMEM((8, 64, 256), bf16),
            pltpu.VMEM((8, 64, 256), bf16),
            dma((2,)), dma((7,)), dma(()), dma((4,)), dma(()), dma(()), dma((CHUNKS,)),
            dma(()), dma(()), dma(()), dma(()), dma((4,)), dma((4,)), dma((8,)), dma((8,)),
            pltpu.SemaphoreType.REGULAR, pltpu.SemaphoreType.REGULAR,
        ],
        compiler_params=pltpu.CompilerParams(
            collective_id=0, has_side_effects=True, vmem_limit_bytes=44 << 20
        ),
        name="joined_attention",
    )(*(pltpu.with_memory_space_constraint(a, pltpu.HBM) for a in operands))


def solution(mesh):
    return jax.shard_map(
        on_device,
        mesh=mesh,
        in_specs=(
            P("slot", None, "row"),
            P("row", "col"),
            P("row", "col"),
            P("row", "col"),
            P("col", "row"),
            P(("slot", "row"), None, None, "col"),
            P(),
            P(),
            P(),
            P("slot", None),
        ),
        out_specs=P("slot", "col", "row"),
        check_vma=False,
    )
```

```python
import functools
import math

import jax
import jax.numpy as jnp
import numpy as np
from jax import lax
from jax.experimental import pallas as pl
from jax.experimental.pallas import tpu as pltpu
from jax.sharding import PartitionSpec as P

HEAD = 128
ROPE_BASE = 500000.0
NEG = -1e30
FAR = 1 << 20
MESH = pl.DeviceIdType.MESH
SCALE = math.log2(math.e) / math.sqrt(HEAD)
f32, bf16, i32 = jnp.float32, jnp.bfloat16, jnp.int32

TOK = 128
NZ, NY, NX = 4, 4, 2
STEPS = NZ * NY * NX
CHUNK = 4
CHUNKS = STEPS // CHUNK
MSG = 32
KEYS = CHUNK * 2 * MSG


def send_order():
    order = [(0, 0, 0), (0, 0, 1)]
    for j in range(1, 4):
        order += [(4 - j, 0, 0), (0, j, 0)]
    for j in range(1, 4):
        order += [(j, 0, 1), (0, j, 1)]
    for m in range(9):
        order += [(*far(m), 1), (*flat(m), 0)]
    return order


def far(m):
    return 1 + (2 * m + 1) % 3, 1 + (m // 3 + m + 2) % 3


def flat(m):
    return 1 + m % 3, 1 + (m // 3 + m) % 3


def kernel(
    hidden, w_query, key_weight, value_weight, w_out, kv_store,
    offset_in, tiles_in, count_in, pos_in, freq_in, steps_in,
    out,
    hid, wq, wk, wv, wo, kv, offs, tiles, count, pos_v, freq_v, steps_v,
    send, recv, ids_v, ids, turn_c, turn_s,
    part_send, part_recv, part_own,
    q, k_new, v_new, owner_sel, pos_m,
    m_s, l_s, acc, att, o_acc, o_send, o_recv,
    load_sem, small_sem, ids_sem, w_sem, self_sem, send_sem, recv_sem,
    pair_send, pair_recv, part_ssem, part_rsem, att_ssem, att_rsem, o_ssem, o_rsem, second_stage, third_stage,
):
    s = lax.axis_index("slot")
    r = lax.axis_index("row")
    c = lax.axis_index("col")
    z, y, x = s // (NY * NX), (s // NX) % NY, s % NX
    me = s * 2 + r
    sign = 1 - 2 * r

    def target(dz, dy, dx):
        return ((z + sign * dz + 4) % 4 * NY + (y + sign * dy + 4) % 4) * NX + (x + dx) % 2

    near = [target(j, 0, 0) for j in range(1, 4)] + [target(0, j, 0) for j in range(1, 4)] + [target(0, 0, 1)]

    barrier = pltpu.get_barrier_semaphore()
    pl.semaphore_signal(barrier, 1, device_id={"row": 1 - r}, device_id_type=MESH)
    pl.semaphore_signal(barrier, 1, device_id={"col": 1 - c}, device_id_type=MESH)
    for slot in near:
        for row in range(2):
            pl.semaphore_signal(barrier, 1, device_id={"slot": slot, "row": row}, device_id_type=MESH)

    def tell(stage):
        for slot in near:
            pl.semaphore_signal(stage, 1, device_id={"slot": slot}, device_id_type=MESH)

    loads = [
        pltpu.make_async_copy(tiles_in.at[:, pl.ds(0, HEAD)], tiles.at[0], small_sem.at[0]),
        pltpu.make_async_copy(tiles_in.at[:, pl.ds(HEAD, HEAD)], tiles.at[1], small_sem.at[4]),
        pltpu.make_async_copy(offset_in, offs, small_sem.at[1]),
        pltpu.make_async_copy(pos_in, pos_v, small_sem.at[2]),
        pltpu.make_async_copy(count_in, count, small_sem.at[5]),
        pltpu.make_async_copy(steps_in, steps_v, small_sem.at[6]),
        pltpu.make_async_copy(freq_in, freq_v, small_sem.at[3]),
    ]
    kv_load = pltpu.make_async_copy(kv_store, kv, load_sem.at[0])
    hid_load = pltpu.make_async_copy(hidden.at[0], hid, load_sem.at[1])
    w_loads = [
        pltpu.make_async_copy(a, b, w_sem.at[n])
        for n, (a, b) in enumerate(((w_query, wq), (key_weight, wk), (value_weight, wv), (w_out, wo)))
    ]
    for copy in loads + [kv_load]:
        copy.start()
    for copy in loads:
        copy.wait()

    lane = lax.broadcasted_iota(i32, (STEPS, HEAD), 1)
    mine_offs = offs[pl.ds(me, 1), :]
    freq = freq_v[...]
    half_sign = jnp.where(lax.broadcasted_iota(i32, (1, HEAD), 1) < HEAD // 2, -1.0, 1.0)
    id_rows = jnp.zeros((STEPS, HEAD), i32)
    for b in range(2):
        block = tiles[b]
        mine = (block >> 7) == me
        code = lane * HEAD + (block & 127)
        picks = (
            jnp.min(jnp.where(mine, code, FAR), axis=1, keepdims=True),
            jnp.max(jnp.where(mine, code, 0), axis=1, keepdims=True),
        )
        for k, pick in enumerate(picks):
            local, tile = pick & 127, pick >> 7
            offset = jnp.sum(jnp.where(lane == local, mine_offs, 0), axis=1, keepdims=True)
            angle = ((b * HEAD + tile) * 8 - offset).astype(f32) * freq
            turn_c[b * 2 + k] = jnp.cos(angle)
            turn_s[b * 2 + k] = jnp.sin(angle) * half_sign
            id_rows = jnp.where(lane == b * 2 + k, local, id_rows)
    ids_v[...] = id_rows
    id_copy = pltpu.make_async_copy(ids_v, ids, ids_sem)
    id_copy.start()
    id_copy.wait()
    kv_load.wait()

    def pack(step, slot):
        for b in range(2):
            for kind in range(2):
                rows = []
                for k in range(2):
                    rows.append(kv[ids[slot, b * 2 + k], kind].astype(f32))
                for h in range(4):
                    heads = []
                    for k in range(2):
                        u = rows[k][:, h * HEAD : (h + 1) * HEAD]
                        if kind == 0:
                            cosine = turn_c[b * 2 + k, pl.ds(slot, 1), :]
                            sine = turn_s[b * 2 + k, pl.ds(slot, 1), :]
                            u = u * cosine + pltpu.roll(u, HEAD // 2, axis=1) * sine
                        heads.append(u)
                    send[step * 2 + h // 2, kind, b * 16 : (b + 1) * 16, (h % 2) * HEAD : (h % 2 + 1) * HEAD] = (
                        jnp.concatenate(heads, axis=0).astype(bf16)
                    )

    pl.semaphore_wait(barrier, 16)
    tell(second_stage)

    pack(0, s)
    self_copy = pltpu.make_async_copy(send.at[r], recv.at[r], self_sem)
    self_copy.start()
    pair_copy = pltpu.make_async_remote_copy(
        send.at[1 - r], recv.at[r], pair_send, pair_recv, device_id={"row": 1 - r}, device_id_type=MESH
    )
    pair_copy.start()

    def ship(step, dz, dy, dx):
        slot = target(dz, dy, dx)
        pack(step, slot)
        for row in range(2):
            pltpu.make_async_remote_copy(
                send.at[step * 2 + row],
                recv.at[step * 2 + r],
                send_sem,
                recv_sem.at[step // CHUNK],
                device_id={"slot": slot, "row": row},
                device_id_type=MESH,
            ).start()

    def ship_one(j, carry):
        ship(2 * j, 4 - j, 0, 0)
        ship(2 * j + 1, 0, j, 0)
        return carry

    def ship_two(j, carry):
        ship(2 * j + 6, j, 0, 1)
        ship(2 * j + 7, 0, j, 1)
        return carry

    def ship_rest(m, carry):
        ship(2 * m + 14, *far(m), 1)
        ship(2 * m + 15, *flat(m), 0)
        return carry

    ship(1, 0, 0, 1)
    lax.fori_loop(1, 4, ship_one, 0)
    pl.semaphore_wait(second_stage, 7)
    tell(third_stage)
    lax.fori_loop(1, 4, ship_two, 0)
    pl.semaphore_wait(third_stage, 7)
    lax.fori_loop(0, 9, ship_rest, 0)

    for copy in [hid_load] + w_loads:
        copy.start()
    hid_load.wait()
    for copy in w_loads[:3]:
        copy.wait()
    x_in = hid[...]

    def project(side, into):
        def body(n, carry):
            cols = pl.ds(pl.multiple_of(side * 1024 + n * 256, 256), 256)
            into[:, pl.ds(pl.multiple_of(n * 256, 256), 256)] = jnp.dot(
                x_in, wq[:, cols], preferred_element_type=f32
            )
            return carry

        lax.fori_loop(0, 4, body, 0)
        cols = pl.ds(pl.multiple_of(side * 256, 256), 256)
        into[:, 1024:1280] = jnp.dot(x_in, wk[:, cols], preferred_element_type=f32)
        into[:, 1280:1536] = jnp.dot(x_in, wv[:, cols], preferred_element_type=f32)

    project(1 - r, part_send)
    part_copy = pltpu.make_async_remote_copy(
        part_send, part_recv, part_ssem, part_rsem, device_id={"row": 1 - r}, device_id_type=MESH
    )
    part_copy.start()
    project(r, part_own)

    def column(row_vector):
        return jnp.transpose(jnp.broadcast_to(row_vector, (HEAD, HEAD)))

    pos_col = column(pos_v[...])
    pos_m[:, :HEAD] = pos_col
    pos_m[:, HEAD:] = pos_col
    owner_cols = [column(tiles[b, pl.ds(s, 1), :] >> 7) for b in range(2)]
    block_of = (lax.broadcasted_iota(i32, (TOK, HEAD), 1) >> 4) & 1
    picked = jnp.where(block_of == 0, owner_cols[0], owner_cols[1])
    owner_sel[:, :HEAD] = picked
    owner_sel[:, HEAD:] = picked
    token_angle = pos_col.astype(f32) * freq
    token_c = jnp.cos(token_angle)
    token_s = jnp.sin(token_angle) * half_sign

    part_copy.wait()

    def total(lo):
        return part_own[:, lo : lo + HEAD] + part_recv[:, lo : lo + HEAD]

    def turned(lo):
        u = total(lo)
        return (u * token_c + pltpu.roll(u, HEAD // 2, axis=1) * token_s).astype(bf16)

    for h in range(8):
        q[h] = turned(h * HEAD)
    for h in range(2):
        k_new[:, h * HEAD : (h + 1) * HEAD] = turned(1024 + h * HEAD)
        v_new[:, h * HEAD : (h + 1) * HEAD] = total(1280 + h * HEAD).astype(bf16)

    def scores(qh, kh, mask):
        sc = lax.dot_general(qh, kh, (((1,), (1,)), ((), ())), preferred_element_type=f32)
        return jnp.where(mask, sc * SCALE, NEG)

    fresh = lax.broadcasted_iota(i32, (TOK, TOK), 1) <= lax.broadcasted_iota(i32, (TOK, TOK), 0)
    for h in range(8):
        g = h // 4
        sc = scores(q[h], k_new[:, g * HEAD : (g + 1) * HEAD], fresh)
        peak = jnp.max(sc, axis=1, keepdims=True)
        p = jnp.exp2(sc - peak)
        m_s[h] = jnp.broadcast_to(peak, (TOK, HEAD))
        l_s[h] = jnp.broadcast_to(jnp.sum(p, axis=1, keepdims=True), (TOK, HEAD))
        acc[h] = jnp.dot(p.astype(bf16), v_new[:, g * HEAD : (g + 1) * HEAD], preferred_element_type=f32)

    limit = count[s] * 8
    lane2 = lax.broadcasted_iota(i32, (1, KEYS), 1)
    src = lane2 >> 5
    in_block, second, unit = (lane2 >> 4) & 1, (lane2 >> 3) & 1, lane2 & 7
    src_row = src & 1
    src_sign = 1 - 2 * src_row
    tile_row = lax.broadcasted_iota(i32, (TOK, KEYS), 0)

    def attend(n, done=None):
        code = steps_v[n : n + 1, :]
        dz, dy, dx = code >> 4, (code >> 2) & 3, code & 1
        source = ((((z - src_sign * dz + 4) & 3) * NY + ((y - src_sign * dy + 4) & 3)) * NX + ((x + dx) & 1)) * 2 + src_row
        here = owner_sel[...] == source
        first = jnp.min(jnp.where(here, tile_row, FAR), axis=0, keepdims=True)
        last = jnp.max(jnp.where(here, tile_row, 0), axis=0, keepdims=True)
        key_pos = (in_block * HEAD + jnp.where(second == 0, first, last)) * 8 + unit
        pos = pos_m[...]
        redone = jnp.max(jnp.where(pos == key_pos, 1, 0), axis=0, keepdims=True)
        key_pos = jnp.where(jnp.logical_or(redone > 0, key_pos >= limit), FAR, key_pos)
        mask = key_pos <= pos
        for g in range(2):
            kh = recv[pl.ds(n * 8, 8), 0, :, g * HEAD : (g + 1) * HEAD].reshape(KEYS, HEAD)
            vh = recv[pl.ds(n * 8, 8), 1, :, g * HEAD : (g + 1) * HEAD].reshape(KEYS, HEAD)
            for j in range(4):
                h = g * 4 + j
                sc = scores(q[h], kh, mask)
                old = m_s[h]
                peak = jnp.maximum(old, jnp.max(sc, axis=1, keepdims=True))
                p = jnp.exp2(sc - jnp.concatenate([peak, peak], axis=1))
                shrink = jnp.exp2(old - peak)
                m_s[h] = peak
                l_s[h] = l_s[h] * shrink + jnp.sum(p, axis=1, keepdims=True)
                acc[h] = acc[h] * shrink + jnp.dot(p.astype(bf16), vh, preferred_element_type=f32)
                if done is not None:
                    done(h)

    def landed(first, many, sem):
        return pltpu.make_async_copy(
            recv.at[pl.ds(first, many)], recv.at[pl.ds(first, many)], sem
        )

    def att_copy(n):
        part = att.at[r]
        return pltpu.make_async_remote_copy(
            part, part, att_ssem.at[n], att_rsem.at[n], device_id={"row": 1 - r}, device_id_type=MESH
        )

    def share(h):
        att[r, :, h * HEAD : (h + 1) * HEAD] = (acc[h] / l_s[h]).astype(bf16)
        if h == 7:
            att_copy(0).start()

    self_copy.wait()
    pair_copy.wait()
    for n in range(CHUNKS):
        if n == 0:
            landed(2, 6, recv_sem.at[0]).wait()
        else:
            landed(8 * n, 8, recv_sem.at[n]).wait()
        attend(n)

    for h in range(8):
        share(h)
    w_loads[3].wait()

    def out_cols(n):
        return pl.ds(pl.multiple_of(n * 256, 256), 256)

    att_copy(0).wait()

    def o_copy(n):
        return pltpu.make_async_remote_copy(
            o_send.at[n], o_recv.at[n], o_ssem.at[n], o_rsem.at[n], device_id={"col": 1 - c}, device_id_type=MESH
        )

    def out_project(n, carry):
        o_acc[:, out_cols(n)] = jnp.dot(att[0], wo[:1024, out_cols(n)], preferred_element_type=f32) + jnp.dot(
            att[1], wo[1024:, out_cols(n)], preferred_element_type=f32
        )
        o_send[n] = o_acc[pl.ds(pl.multiple_of((1 - c) * 64, 64), 64), out_cols(n)].astype(bf16)
        o_copy(n).start()
        return carry

    own_rows = pl.ds(pl.multiple_of(c * 64, 64), 64)
    lax.fori_loop(0, 8, out_project, 0)

    def finish(n, carry):
        o_copy(n).wait()
        out[0, :, out_cols(n)] = (o_acc[own_rows, out_cols(n)] + o_recv[n].astype(f32)).astype(bf16)
        return carry

    lax.fori_loop(0, 8, finish, 0)
    pltpu.make_async_copy(send.at[pl.ds(2, 62)], send.at[pl.ds(2, 62)], send_sem).wait()


def on_device(
    hidden, w_query, key_weight, value_weight, w_out, kv_store,
    stretch_offset, tile_stretch, slot_count, recomp_pos,
):
    freq = (ROPE_BASE ** (-2.0 * np.arange(HEAD // 2, dtype=np.float32) / HEAD)).astype(np.float32)
    freq = jnp.asarray(np.concatenate([freq, freq])[None, :])
    steps = np.repeat([dz * 16 + dy * 4 + dx for dz, dy, dx in send_order()], 2 * MSG).reshape(CHUNKS, KEYS)
    steps = jnp.asarray(steps, i32)
    dma = pltpu.SemaphoreType.DMA
    operands = (
        hidden, w_query, key_weight, value_weight, w_out, kv_store,
        stretch_offset.reshape(64, 128), tile_stretch, slot_count, recomp_pos, freq, steps,
    )
    return pl.pallas_call(
        kernel,
        out_shape=jax.ShapeDtypeStruct((1, 64, 2048), bf16),
        in_specs=[pl.BlockSpec(memory_space=pltpu.HBM)] * 12,
        out_specs=pl.BlockSpec(memory_space=pltpu.VMEM),
        scratch_shapes=[
            pltpu.VMEM((TOK, 2048), bf16),
            pltpu.VMEM((2048, 2048), bf16),
            pltpu.VMEM((2048, 512), bf16),
            pltpu.VMEM((2048, 512), bf16),
            pltpu.VMEM((2048, 2048), bf16),
            pltpu.VMEM((128, 2, 8, 512), bf16),
            pltpu.VMEM((64, 128), i32),
            pltpu.VMEM((2, 32, 128), i32),
            pltpu.SMEM((32,), i32),
            pltpu.VMEM((1, 128), i32),
            pltpu.VMEM((1, 128), f32),
            pltpu.VMEM((CHUNKS, KEYS), i32),
            pltpu.VMEM((2 * STEPS, 2, MSG, 256), bf16),
            pltpu.VMEM((2 * STEPS, 2, MSG, 256), bf16),
            pltpu.VMEM((STEPS, HEAD), i32),
            pltpu.SMEM((STEPS, HEAD), i32),
            pltpu.VMEM((4, STEPS, HEAD), f32),
            pltpu.VMEM((4, STEPS, HEAD), f32),
            pltpu.VMEM((TOK, 1536), f32),
            pltpu.VMEM((TOK, 1536), f32),
            pltpu.VMEM((TOK, 1536), f32),
            pltpu.VMEM((8, TOK, HEAD), bf16),
            pltpu.VMEM((TOK, 256), bf16),
            pltpu.VMEM((TOK, 256), bf16),
            pltpu.VMEM((TOK, KEYS), i32),
            pltpu.VMEM((TOK, KEYS), i32),
            pltpu.VMEM((8, TOK, HEAD), f32),
            pltpu.VMEM((8, TOK, HEAD), f32),
            pltpu.VMEM((8, TOK, HEAD), f32),
            pltpu.VMEM((2, TOK, 1024), bf16),
            pltpu.VMEM((TOK, 2048), f32),
            pltpu.VMEM((8, 64, 256), bf16),
            pltpu.VMEM((8, 64, 256), bf16),
            dma((2,)), dma((7,)), dma(()), dma((4,)), dma(()), dma(()), dma((CHUNKS,)),
            dma(()), dma(()), dma(()), dma(()), dma((4,)), dma((4,)), dma((8,)), dma((8,)),
            pltpu.SemaphoreType.REGULAR, pltpu.SemaphoreType.REGULAR,
        ],
        compiler_params=pltpu.CompilerParams(
            collective_id=0, has_side_effects=True, vmem_limit_bytes=44 << 20
        ),
        name="joined_attention",
    )(*(pltpu.with_memory_space_constraint(a, pltpu.HBM) for a in operands))


def solution(mesh):
    return jax.shard_map(
        on_device,
        mesh=mesh,
        in_specs=(
            P("slot", None, "row"),
            P("row", "col"),
            P("row", "col"),
            P("row", "col"),
            P("col", "row"),
            P(("slot", "row"), None, None, "col"),
            P(),
            P(),
            P(),
            P("slot", None),
        ),
        out_specs=P("slot", "col", "row"),
        check_vma=False,
    )
```
